256 devices in a mesh: seq: 32 (over y, z), head: 8 (over x, core).
Axes of the slice: x: 4, y: 4, z: 8, core: 2. Of those that a mesh axis runs over, the one named last changes fastest.
Arguments:
- hidden: bfloat16 [16384, 8192], P('seq', 'head'), may hold values from -6 to 6
- gain: float32 [8192], replicated, may hold values from 0.25 to 1.75
- key_matrix: bfloat16 [8192, 1024], P(None, 'head'), may hold values from -0.0625 to 0.0625
- value_matrix: bfloat16 [8192, 1024], P(None, 'head'), may hold values from -0.0625 to 0.0625
- queries: bfloat16 [64, 8192], P(None, 'head'), may hold values from -360 to 360
- window_len: int32 [8], P('head'), may hold values from 16 to 64, as said below
- kernel_width: int32 [8], P('head'), may hold values from 1 to 15, as said below
- kept_block_count: int32 [8], P('head'), may hold values from 1 to 64
Outputs:
- block_scores: float32 [8, 128], P('head', 'seq')
- kept_fraction: float32 [8], P('head')
The draws below stay inside these ranges and needn't reach their ends.
Inputs may be any that keep to these rules, and one draw needn't show every extreme that they name: `window_len`: at least one key-value head uses all 64 window queries. `kernel_width`: odd; at least one key-value head has width 15.
All inputs are finite; a program needn't handle non-finite values.
Results may differ from the reference program's by a relative error of at most 0.0112.
The reference program's roundings to bfloat16 on the way (of `normed` and `keys`) count: a program that leaves them out, or rounds other values in their place, can miss the bound.
Values may be sent and summed in bfloat16 or wider, within the bound.
A program may use at most 128 MiB of HBM per device.

```python
import jax
import jax.numpy as jnp
from jax import lax

MODEL_WIDTH = 8192
HEAD_DIMENSION = 128
QUERY_PER_GROUP = 8
WINDOW_QUERIES = 64
BLK = 128
KERNEL_LIMIT = 15
KEY_VALUE_HEADS = 8
H = 64
PROMPT_TOKENS = 16384
KEY_BLOCK_COUNT = 128
N_SEQ = 32


def draw_queries(key, part):
    leading_part = jax.random.fold_in(jax.random.fold_in(key, 7), 0)
    base = jax.random.truncated_normal(leading_part, -6.0, 6.0, (WINDOW_QUERIES, H * HEAD_DIMENSION), jnp.float32)
    return base.astype(jnp.bfloat16)


def draw_window_len(key, part):
    leading_part, trailing_part = jax.random.split(jax.random.fold_in(key, 11))
    value_rows = jax.random.randint(leading_part, (KEY_VALUE_HEADS,), WINDOW_QUERIES // 4, WINDOW_QUERIES + 1)
    selected_blocks = jax.random.randint(trailing_part, (), 0, KEY_VALUE_HEADS)
    return jnp.where(jnp.arange(KEY_VALUE_HEADS) == selected_blocks, WINDOW_QUERIES, value_rows).astype(jnp.int32)


def draw_kernel_width(key, part):
    leading_part, trailing_part = jax.random.split(jax.random.fold_in(key, 13))
    kernel_halfspan = jax.random.randint(leading_part, (KEY_VALUE_HEADS,), 0, (KERNEL_LIMIT - 1) // 2 + 1)
    selected_blocks = jax.random.randint(trailing_part, (), 0, KEY_VALUE_HEADS)
    return jnp.where(jnp.arange(KEY_VALUE_HEADS) == selected_blocks, KERNEL_LIMIT, 2 * kernel_halfspan + 1).astype(jnp.int32)


def set_ends(values, key, smallest, top_value):
    longest = values.shape.index(max(values.shape))
    spots = []
    for shift in (0, 1):
        where = [jax.random.randint(jax.random.fold_in(key, axis), (), 0, length) for axis, length in enumerate(values.shape)]
        where[longest] = (where[longest] + shift) % values.shape[longest]
        spots.append(tuple(where))
    return values.at[spots[0]].set(smallest).at[spots[1]].set(top_value)


def shard_levels(own_key, shape, pieces, least, top_value):
    level = 1.0
    for position, parts in pieces:
        draws = jax.random.uniform(jax.random.fold_in(jax.random.fold_in(own_key, 6), position), (parts,), jnp.float32, least / len(pieces), top_value / len(pieces))
        level = level * jnp.repeat(jnp.exp(draws), shape[position] // parts).reshape((-1,) + (1,) * (len(shape) - 1 - position))
    return level


def scatter_about(rng, shape, spread, most, pieces=(), held_as=jnp.bfloat16):
    drawn = spread * jax.random.normal(rng, shape, jnp.float32)
    if pieces:
        drawn = drawn * shard_levels(rng, shape, pieces, -0.22, 0.18)
    return jnp.clip(drawn, -most, most).astype(held_as)


def setup_inputs(seed: int = 0) -> dict:
    streams_of = jax.random.split(jax.random.key(seed), 9)
    hidden = scatter_about(streams_of[0], (PROMPT_TOKENS, MODEL_WIDTH), 1.0, 6.0, ((0, 32), (1, 8)))
    gain = jnp.clip(1.0 + 0.15 * jax.random.normal(streams_of[1], (MODEL_WIDTH,), jnp.float32), 0.25, 1.75)
    key_matrix = scatter_about(streams_of[2], (MODEL_WIDTH, KEY_VALUE_HEADS * HEAD_DIMENSION), MODEL_WIDTH ** -0.5, 0.0625, ((1, 8),))
    value_matrix = scatter_about(streams_of[3], (MODEL_WIDTH, KEY_VALUE_HEADS * HEAD_DIMENSION), MODEL_WIDTH ** -0.5, 0.0625, ((1, 8),))
    queries = draw_queries(jax.random.fold_in(streams_of[8], 71), 0)
    window_len = draw_window_len(jax.random.fold_in(streams_of[8], 71), 0)
    kernel_width = draw_kernel_width(jax.random.fold_in(streams_of[8], 71), 0)
    kept_block_count = set_ends(jax.random.randint(streams_of[7], (KEY_VALUE_HEADS,), 1, KEY_BLOCK_COUNT // 2 + 1), jax.random.fold_in(streams_of[7], 1), 1, (KEY_BLOCK_COUNT // 2 + 1) - 1).astype(jnp.int32)
    return {"hidden": hidden, "gain": gain, "key_matrix": key_matrix, "value_matrix": value_matrix, "queries": queries, "window_len": window_len, "kernel_width": kernel_width, "kept_block_count": kept_block_count}


def rotate(raw, positions):
    half = raw.shape[1] // 2
    freq = 500000.0 ** (-(jnp.arange(half).astype(jnp.float32) * 2.0) / raw.shape[1])
    angle = positions[:, None] * freq[None, :]
    leading_part = raw[:, :half]
    trailing_part = raw[:, half:]
    return jnp.concatenate([leading_part * jnp.cos(angle) - trailing_part * jnp.sin(angle), trailing_part * jnp.cos(angle) + leading_part * jnp.sin(angle)], axis=1)

def reference(hidden, gain, key_matrix, value_matrix, queries, window_len, kernel_width, kept_block_count):

    def project(rows):
        floats = rows.astype(jnp.float32)
        meansq = lax.optimization_barrier(jnp.mean(floats * floats, axis=1))
        normed = (floats * gain[None, :]).astype(jnp.bfloat16)
        scale = lax.rsqrt(meansq + 1e-05)[:, None]
        kproj = jnp.dot(normed, key_matrix, preferred_element_type=jnp.float32) * scale
        vproj = jnp.dot(normed, value_matrix, preferred_element_type=jnp.float32) * scale
        return (kproj, vproj)
    blocks = hidden.reshape(N_SEQ, PROMPT_TOKENS // N_SEQ, MODEL_WIDTH)
    key_states_full, value_states_full = lax.map(project, blocks)
    key_states_full = key_states_full.reshape(PROMPT_TOKENS, KEY_VALUE_HEADS, HEAD_DIMENSION).transpose(1, 0, 2)
    value_states_full = value_states_full.reshape(PROMPT_TOKENS, KEY_VALUE_HEADS, HEAD_DIMENSION).transpose(1, 0, 2)
    query_states_full = queries.reshape(WINDOW_QUERIES, KEY_VALUE_HEADS, QUERY_PER_GROUP, HEAD_DIMENSION).transpose(1, 0, 2, 3).reshape(KEY_VALUE_HEADS, WINDOW_QUERIES * QUERY_PER_GROUP, HEAD_DIMENSION)
    positions = jnp.arange(PROMPT_TOKENS).astype(jnp.float32)
    tokidx = jnp.arange(PROMPT_TOKENS).astype(jnp.int32)
    reach = (KERNEL_LIMIT - 1) // 2

    def per_group(items):
        kraw, vraw, qrows, wlen, kwidth, keep = items
        keys = rotate(kraw, positions).astype(jnp.bfloat16)
        vmag = lax.optimization_barrier(jnp.mean(jnp.abs(vraw), axis=1))
        scores = lax.dot_general(qrows, keys, (((1,), (1,)), ((), ())), preferred_element_type=jnp.float32) * HEAD_DIMENSION ** (-0.5)
        limit = jnp.repeat(PROMPT_TOKENS - WINDOW_QUERIES + jnp.arange(WINDOW_QUERIES).astype(jnp.int32), QUERY_PER_GROUP)
        allowed = tokidx[None, :] <= limit[:, None]
        scores = jnp.where(allowed, scores, jnp.float32(-1e+30))
        top = lax.optimization_barrier(jnp.max(scores, axis=1))
        expo = jnp.exp(scores - top[:, None])
        total = lax.optimization_barrier(jnp.sum(expo, axis=1))
        used = (jnp.arange(WINDOW_QUERIES).astype(jnp.int32) >= WINDOW_QUERIES - wlen).astype(jnp.float32)
        rowwt = jnp.repeat(used, QUERY_PER_GROUP) / total
        column = jnp.dot(rowwt, expo, precision=lax.Precision.HIGHEST) * vmag
        padded = jnp.pad(column, reach)
        kernel_halfspan = (kwidth - 1) // 2
        pooled = column
        for shift in range(1, reach + 1):
            wider = jnp.maximum(jnp.maximum(pooled, padded[reach + shift:reach + shift + PROMPT_TOKENS]), padded[reach - shift:reach - shift + PROMPT_TOKENS])
            pooled = jnp.where(shift <= kernel_halfspan, wider, pooled)
        scored = lax.optimization_barrier(jnp.sum(pooled.reshape(KEY_BLOCK_COUNT, BLK), axis=1))
        ordered = -jnp.sort(-scored)
        ranks = jnp.arange(KEY_BLOCK_COUNT).astype(jnp.int32)
        kept = jnp.sum(jnp.where(ranks < keep, ordered, jnp.float32(0.0)))
        return (scored, kept / jnp.sum(scored))
    block_scores, kept_fraction = lax.map(per_group, (key_states_full, value_states_full, query_states_full, window_len, kernel_width, kept_block_count))
    return (block_scores, kept_fraction)
```

```python
import functools

import jax
import jax.numpy as jnp
import numpy as np
from jax import lax
from jax.experimental import pallas as pl
from jax.experimental.pallas import tpu as pltpu
from jax.sharding import PartitionSpec as P

MESH = pl.DeviceIdType.MESH
BLK = 128
KERNEL_LIMIT = 15
NX = 4
CHUNKS = 8
NEG = -1e30


def kernel(
    n_seq,
    hid, gain, wk, wv, q, wlen, kwidth, keep, freq,
    blocks_out, frac_out,
    hbuf, w, qs, cos_t, sin_t, acc, ssq, vmag, ex, stat, gt, ext, halo_p,
    halo_send, halo_recv, stat_recv, blk_recv,
    load_sem, own_send, fwd_send, d2d_own_send, d2d_send, recv_sem,
    halo_ssem, halo_rsem, stat_ssem, stat_rsem, blk_ssem, blk_rsem,
):
    tok = hid.shape[0]
    feat = hid.shape[1]
    hd = wk.shape[1]
    window = q.shape[0]
    group = q.shape[1] // hd
    nq = window * group
    nb = tok // BLK
    rows = tok // CHUNKS
    half = CHUNKS // 2
    full_width = gain.shape[1]
    total_tokens = tok * n_seq

    s = lax.axis_index("seq")
    h = lax.axis_index("head")
    x, c = h // 2, lax.rem(h, 2)
    xr, xl, xo = lax.rem(x + 1, NX), lax.rem(x + 3, NX), lax.rem(x + 2, NX)
    right = {"seq": s, "head": xr * 2 + c}
    left = {"seq": s, "head": xl * 2 + c}
    partner = {"seq": s, "head": x * 2 + 1 - c}
    seq_next = {"seq": lax.rem(s + 1, n_seq), "head": h}
    seq_prev = {"seq": lax.rem(s + n_seq - 1, n_seq), "head": h}

    src = [x * 2 + c, xl * 2 + c, xr * 2 + c, xo * 2 + c]
    src += [x * 2 + 1 - c, xl * 2 + 1 - c, xr * 2 + 1 - c, xo * 2 + 1 - c]

    loads = [
        pltpu.make_async_copy(hid, hbuf.at[0], load_sem.at[0]),
        pltpu.make_async_copy(wk, w.at[:, 0:hd], load_sem.at[1]),
        pltpu.make_async_copy(wv, w.at[:, hd : 2 * hd], load_sem.at[2]),
    ]
    for cp in loads:
        cp.start()

    barrier = pltpu.get_barrier_semaphore()
    for dev in (right, left, partner):
        pl.semaphore_signal(barrier, inc=1, device_id=dev, device_id_type=MESH)

    def greet(d, carry):
        dev = {"seq": lax.rem(s + d, n_seq), "head": h}
        pl.semaphore_signal(barrier, inc=1, device_id=dev, device_id_type=MESH)
        return carry

    lax.fori_loop(1, n_seq, greet, 0)
    pl.semaphore_wait(barrier, 3 + n_seq - 1)

    def part(k):
        return slice(k * rows, (k + 1) * rows)

    def send(source, slot, k, ssem, dev):
        return pltpu.make_async_remote_copy(
            src_ref=source, dst_ref=hbuf.at[slot, part(k)], send_sem=ssem,
            recv_sem=recv_sem.at[slot, k], device_id=dev, device_id_type=MESH,
        )

    started = []

    def go(cp):
        cp.start()
        started.append(cp)

    for k in range(CHUNKS):
        go(send(hid.at[part(k)], 1, k, own_send.at[0, k], right))
        go(send(hid.at[part(k)], 2, k, own_send.at[1, k], left))
    for k in range(CHUNKS):
        go(send(hid.at[part(k)], 4, k, d2d_own_send.at[k], partner))

    def landed(slot, k):
        send(hbuf.at[slot, part(k)], slot, k, own_send.at[0, 0], right).wait_recv()

    for b in range(nb):
        position = (s * tok + b * BLK + lax.broadcasted_iota(jnp.int32, (BLK, hd), 0)).astype(jnp.float32)
        angle = position * freq[0:1, :]
        lane = lax.broadcasted_iota(jnp.int32, (BLK, hd), 1)
        cos_t[b * BLK : (b + 1) * BLK, :] = jnp.cos(angle)
        sine = jnp.sin(angle)
        sin_t[b * BLK : (b + 1) * BLK, :] = jnp.where(lane < hd // 2, -sine, sine)
    for j in range(group):
        qs[j * window : (j + 1) * window, :] = q[:, j * hd : (j + 1) * hd]
    for cp in loads:
        cp.wait()

    def accumulate(slot, first, count, size, fresh=False):
        head = src[slot]
        offset = pl.multiple_of(head * feat, feat)

        def body(i, carry):
            at = pl.ds(pl.multiple_of(first + i * size, size), size)
            block = hbuf[slot, at, :].astype(jnp.float32)
            normed = (block * gain[0:1, pl.ds(offset, feat)]).astype(jnp.bfloat16)
            product = jnp.dot(normed, w[pl.ds(offset, feat), :], preferred_element_type=jnp.float32)
            square = block * block
            lanes = square[:, 0:128]
            for t in range(1, feat // 128):
                lanes = lanes + square[:, t * 128 : (t + 1) * 128]
            if fresh:
                acc[at, :] = product
                ssq[at, :] = lanes
            else:
                acc[at, :] += product
                ssq[at, :] += lanes
            return carry

        lax.fori_loop(0, count, body, 0)

    accumulate(0, 0, nb, BLK, fresh=True)
    for k in range(CHUNKS):
        landed(4, k)
    accumulate(4, 0, nb, BLK)

    per = BLK // rows
    for b in range(nb):
        for k in range(b * per, (b + 1) * per):
            landed(1, k)
            if k < half:
                go(send(hbuf.at[1, part(k)], 3, k, fwd_send.at[k], right))
            go(send(hbuf.at[1, part(k)], 5, k, d2d_send.at[0, k], partner))
            landed(2, k)
            if k >= half:
                go(send(hbuf.at[2, part(k)], 3, k, fwd_send.at[k], left))
            go(send(hbuf.at[2, part(k)], 6, k, d2d_send.at[1, k], partner))
        accumulate(1, b * BLK, 1, BLK)
        accumulate(2, b * BLK, 1, BLK)
        for k in range(b * per, (b + 1) * per):
            landed(5, k)
            landed(6, k)
        accumulate(5, b * BLK, 1, BLK)
        accumulate(6, b * BLK, 1, BLK)

    lane_q = lax.broadcasted_iota(jnp.int32, (1, nq), 1)
    limit = total_tokens - window + lax.rem(lane_q, window)

    def scores_of(keys):
        return lax.dot_general(
            keys, qs[...], (((1,), (1,)), ((), ())), preferred_element_type=jnp.float32
        ) * hd ** (-0.5)

    def halo_copy(side, dev):
        return pltpu.make_async_remote_copy(
            src_ref=halo_send.at[side], dst_ref=halo_recv.at[side], send_sem=halo_ssem.at[side],
            recv_sem=halo_rsem.at[side], device_id=dev, device_id_type=MESH,
        )

    def finish(b):
        at = slice(b * BLK, (b + 1) * BLK)
        meansq = jnp.sum(ssq[at, :], axis=1, keepdims=True) / full_width
        inv = lax.rsqrt(meansq + 1e-05)
        kraw = acc[at, 0:hd] * inv
        vraw = acc[at, hd : 2 * hd] * inv
        keys = (kraw * cos_t[at, :] + pltpu.roll(kraw, hd // 2, 1) * sin_t[at, :]).astype(jnp.bfloat16)
        mag = jnp.sum(jnp.abs(vraw), axis=1, keepdims=True) / hd
        mag = jnp.broadcast_to(mag, (BLK, 128))
        vmag[at, :] = mag
        if b == 0:
            halo_send[0, 0] = keys[0:16, :].astype(jnp.float32)
            halo_send[0, 1] = mag[0:16, :]
            go(halo_copy(0, seq_prev))
        if b == nb - 1:
            halo_send[1, 0] = keys[BLK - 16 :, :].astype(jnp.float32)
            halo_send[1, 1] = mag[BLK - 16 :, :]
            go(halo_copy(1, seq_next))
        scores = scores_of(keys)
        token = s * tok + b * BLK + lax.broadcasted_iota(jnp.int32, (BLK, nq), 0)
        scores = jnp.where(token <= limit, scores, NEG)
        top = jnp.max(scores, axis=0, keepdims=True)
        expo = jnp.exp(scores - top)
        ex[at, :] = expo
        tot = jnp.sum(expo, axis=0, keepdims=True)
        for j in range(nq // 128):
            stat[b, j : j + 1, :] = top[:, j * 128 : (j + 1) * 128]
            stat[b, 4 + j : 5 + j, :] = tot[:, j * 128 : (j + 1) * 128]

    for k in range(half):
        landed(3, k)
        go(send(hbuf.at[3, part(k)], 7, k, d2d_send.at[2, k], partner))
        landed(3, half + k)
        go(send(hbuf.at[3, part(half + k)], 7, half + k, d2d_send.at[2, half + k], partner))
        if (k + 1) % per == 0:
            i = k // per
            for b in (i, nb // 2 + i):
                accumulate(3, b * BLK, 1, BLK)
                for m in range(b * per, (b + 1) * per):
                    landed(7, m)
                accumulate(7, b * BLK, 1, BLK)
                finish(b)

    merged = stat[0]
    for b in range(1, nb):
        other = stat[b]
        top = jnp.maximum(merged, other)
        scaled = pltpu.roll(jnp.exp(merged - top), 4, 0) * merged + pltpu.roll(jnp.exp(other - top), 4, 0) * other
        sub = lax.broadcasted_iota(jnp.int32, (8, 128), 0)
        merged = jnp.where(sub < 4, top, scaled)
    stat_recv[s] = merged

    def stat_copy(d):
        return pltpu.make_async_remote_copy(
            src_ref=stat_recv.at[s], dst_ref=stat_recv.at[s], send_sem=stat_ssem.at[d],
            recv_sem=stat_rsem.at[d], device_id={"seq": lax.rem(s + d, n_seq), "head": h}, device_id_type=MESH,
        )

    def blk_copy(d):
        return pltpu.make_async_remote_copy(
            src_ref=blk_recv.at[s], dst_ref=blk_recv.at[s], send_sem=blk_ssem.at[d],
            recv_sem=blk_rsem.at[d], device_id={"seq": lax.rem(s + d, n_seq), "head": h}, device_id_type=MESH,
        )

    def each_peer(act):
        def body(d, carry):
            act(d)
            return carry

        lax.fori_loop(1, n_seq, body, 0)

    each_peer(lambda d: stat_copy(d).start())

    halo_copy(0, seq_prev).wait_recv()
    halo_copy(1, seq_next).wait_recv()
    edge_keys = jnp.concatenate([halo_recv[0, 0], halo_recv[1, 0]], axis=0).astype(jnp.bfloat16)
    edge_scores = scores_of(edge_keys)
    edge_row = lax.broadcasted_iota(jnp.int32, (32, nq), 0)
    edge_token = jnp.where(edge_row < 16, (s + 1) * tok + edge_row, s * tok - 32 + edge_row)
    edge_ok = (edge_token >= 0) & (edge_token <= limit)
    edge_scores = jnp.where(edge_ok, edge_scores, NEG)
    edge_top = jnp.max(edge_scores, axis=0, keepdims=True)
    edge_expo = jnp.where(edge_ok, jnp.exp(edge_scores - edge_top), 0.0)
    for j in range(nq // 128):
        stat[nb, j : j + 1, :] = edge_top[:, j * 128 : (j + 1) * 128]

    each_peer(lambda d: stat_copy(d).wait_recv())
    everyone = stat_recv[...]
    row_top = jnp.max(everyone, axis=0)
    row_total = jnp.sum(pltpu.roll(jnp.exp(everyone - row_top[None]), 4, 1) * everyone, axis=0)
    row_total = pltpu.roll(row_total, 4, 0)
    sub8 = lax.broadcasted_iota(jnp.int32, (8, 128), 0)
    lane8 = lax.broadcasted_iota(jnp.int32, (8, 128), 1)
    wrow = lax.rem(lane8, window)
    used = (wrow >= window - wlen[0]) & (sub8 < 4)
    for b in range(nb + 1):
        factor = jnp.exp(stat[b] - row_top) / row_total
        gt[b] = jnp.where(used, factor, 0.0)

    def weighted(expo, b):
        total = expo[:, 0:128] * gt[b, 0:1, :]
        for j in range(1, nq // 128):
            total = total + expo[:, j * 128 : (j + 1) * 128] * gt[b, j : j + 1, :]
        return total

    ext[...] = jnp.zeros_like(ext)
    for b in range(nb):
        at = slice(b * BLK, (b + 1) * BLK)
        column = weighted(ex[at, :], b) * vmag[at, :]
        ext[b + 1 : b + 2, :] = jnp.sum(column.T, axis=0, keepdims=True)
    edge = weighted(edge_expo, nb)
    halo_p[...] = jnp.zeros_like(halo_p)
    halo_p[0:16, :] = edge[0:16, :] * halo_recv[0, 1]
    halo_p[BLK - 16 :, :] = edge[16:32, :] * halo_recv[1, 1]
    edge_row_sum = jnp.sum(halo_p[...].T, axis=0, keepdims=True)
    ext[0:1, :] = edge_row_sum
    ext[nb + 1 : nb + 2, :] = edge_row_sum

    here = ext[...]
    before = pltpu.roll(here, 1, 0)
    after = pltpu.roll(here, 7, 0)
    halfspan = (kwidth[0] - 1) // 2
    pooled = here
    for shift in range(1, (KERNEL_LIMIT - 1) // 2 + 1):
        ahead = pltpu.roll(jnp.where(lane8 >= shift, here, after), 128 - shift, 1)
        behind = pltpu.roll(jnp.where(lane8 < 128 - shift, here, before), shift, 1)
        wider = jnp.maximum(jnp.maximum(pooled, ahead), behind)
        pooled = jnp.where(shift <= halfspan, wider, pooled)
    sums = jnp.broadcast_to(jnp.sum(pooled, axis=1, keepdims=True), (8, 128))
    mine = (sub8 >= 1) & (sub8 <= nb)
    local = jnp.sum(jnp.where(mine & (lane8 == sub8 - 1), sums, 0.0), axis=0, keepdims=True)
    blocks_out[...] = local[:, 0:nb]
    placed = jnp.sum(jnp.where(mine & (lane8 == s * nb + sub8 - 1), sums, 0.0), axis=0, keepdims=True)
    blk_recv[s] = jnp.broadcast_to(placed, (8, 128))
    each_peer(lambda d: blk_copy(d).start())
    each_peer(lambda d: blk_copy(d).wait_recv())
    row = jnp.sum(blk_recv[...], axis=0)[0:1, :]
    by_lane = jnp.broadcast_to(row, (128, 128))
    by_sub = by_lane.T
    si = lax.broadcasted_iota(jnp.int32, (128, 128), 0)
    li = lax.broadcasted_iota(jnp.int32, (128, 128), 1)
    larger = (by_sub > by_lane) | ((by_sub == by_lane) & (si < li))
    rank = jnp.sum(larger.astype(jnp.float32), axis=0, keepdims=True)
    kept = jnp.sum(jnp.where(rank < keep[0].astype(jnp.float32), row, 0.0), axis=1, keepdims=True)
    frac_out[...] = kept / jnp.sum(row, axis=1, keepdims=True)

    for cp in started:
        cp.wait_send()
    each_peer(lambda d: stat_copy(d).wait_send())
    each_peer(lambda d: blk_copy(d).wait_send())


def solution(mesh):
    n_seq = mesh.shape["seq"]

    def local(hidden, gain, key_matrix, value_matrix, queries, window_len, kernel_width, kept_block_count):
        tok, feat = hidden.shape
        width, hd = key_matrix.shape
        nq = queries.shape[0] * queries.shape[1] // hd
        nb = tok // BLK
        freq = (500000.0 ** (-(np.arange(hd // 2) * 2.0) / hd)).astype(np.float32)
        freq = jnp.asarray(np.concatenate([freq, freq])[None, :])
        anyspace = pl.BlockSpec(memory_space=pl.ANY)
        vmem = pl.BlockSpec(memory_space=pltpu.VMEM)
        smem = pl.BlockSpec(memory_space=pltpu.SMEM)
        f32, bf16 = jnp.float32, jnp.bfloat16
        dma = pltpu.SemaphoreType.DMA
        blocks, frac = pl.pallas_call(
            functools.partial(kernel, n_seq),
            out_shape=(
                jax.ShapeDtypeStruct((1, nb), f32),
                jax.ShapeDtypeStruct((1, 1), f32),
            ),
            in_specs=[anyspace, vmem, anyspace, anyspace, vmem, smem, smem, smem, vmem],
            out_specs=(vmem, vmem),
            scratch_shapes=[
                pltpu.VMEM((8, tok, feat), bf16),
                pltpu.VMEM((width, 2 * hd), bf16),
                pltpu.VMEM((nq, hd), bf16),
                pltpu.VMEM((tok, hd), f32),
                pltpu.VMEM((tok, hd), f32),
                pltpu.VMEM((tok, 2 * hd), f32),
                pltpu.VMEM((tok, 128), f32),
                pltpu.VMEM((tok, 128), f32),
                pltpu.VMEM((tok, nq), f32),
                pltpu.VMEM((nb + 1, 8, 128), f32),
                pltpu.VMEM((nb + 1, 8, 128), f32),
                pltpu.VMEM((8, 128), f32),
                pltpu.VMEM((BLK, 128), f32),
                pltpu.VMEM((2, 2, 16, 128), f32),
                pltpu.VMEM((2, 2, 16, 128), f32),
                pltpu.VMEM((n_seq, 8, 128), f32),
                pltpu.VMEM((n_seq, 8, 128), f32),
                dma((3,)),
                dma((2, CHUNKS)),
                dma((CHUNKS,)),
                dma((CHUNKS,)),
                dma((3, CHUNKS)),
                dma((8, CHUNKS)),
                dma((2,)),
                dma((2,)),
                dma((n_seq,)),
                dma((n_seq,)),
                dma((n_seq,)),
                dma((n_seq,)),
            ],
            compiler_params=pltpu.CompilerParams(
                collective_id=0, has_side_effects=True, vmem_limit_bytes=56 * 1024 * 1024
            ),
        )(
            hidden, gain.reshape(1, -1), key_matrix, value_matrix, queries,
            window_len, kernel_width, kept_block_count, freq,
        )
        return blocks, frac.reshape(1)

    return jax.shard_map(
        local,
        mesh=mesh,
        in_specs=(
            P("seq", "head"), P(), P(None, "head"), P(None, "head"), P(None, "head"),
            P("head"), P("head"), P("head"),
        ),
        out_specs=(P("head", "seq"), P("head")),
        check_vma=False,
    )
```

```python
import functools

import jax
import jax.numpy as jnp
import numpy as np
from jax import lax
from jax.experimental import pallas as pl
from jax.experimental.pallas import tpu as pltpu
from jax.sharding import PartitionSpec as P

MESH = pl.DeviceIdType.MESH
BLK = 128
KERNEL_LIMIT = 15
NX = 4
N_Z = 8
CHUNKS = 8
NEG = -1e30


def kernel(
    n_seq,
    hid, gain, wk, wv, q, wlen_in, kwidth_in, keep_in, freq,
    blocks_out, frac_out,
    hbuf, w, qs, cos_t, sin_t, acc, ssq, vmag, ex, stat, gt, ext, halo_p,
    halo_send, halo_recv, stat_recv, blk_recv, wlen, kwidth, keep,
    load_sem, own_send, fwd_send, d2d_own_send, d2d_send, recv_sem,
    halo_ssem, halo_rsem, stat_ssem, stat_rsem, blk_ssem, blk_rsem, met,
):
    tok = hid.shape[0]
    feat = hid.shape[1]
    hd = wk.shape[1]
    window = q.shape[0]
    group = q.shape[1] // hd
    nq = window * group
    nb = tok // BLK
    rows = tok // CHUNKS
    half = CHUNKS // 2
    full_width = gain.shape[1]
    total_tokens = tok * n_seq

    s = lax.axis_index("seq")
    h = lax.axis_index("head")
    x, c = h // 2, lax.rem(h, 2)
    n_z = N_Z
    n_y = n_seq // N_Z
    y, z = s // n_z, lax.rem(s, n_z)
    xr, xl, xo = lax.rem(x + 1, NX), lax.rem(x + 3, NX), lax.rem(x + 2, NX)
    right = {"seq": s, "head": xr * 2 + c}
    left = {"seq": s, "head": xl * 2 + c}
    partner = {"seq": s, "head": x * 2 + 1 - c}
    seq_next = {"seq": lax.rem(s + 1, n_seq), "head": h}
    seq_prev = {"seq": lax.rem(s + n_seq - 1, n_seq), "head": h}

    src = [x * 2 + c, xl * 2 + c, xr * 2 + c, xo * 2 + c]
    src += [x * 2 + 1 - c, xl * 2 + 1 - c, xr * 2 + 1 - c, xo * 2 + 1 - c]

    loads = [
        pltpu.make_async_copy(hid, hbuf.at[0], load_sem.at[0]),
        pltpu.make_async_copy(wk, w.at[:, 0:hd], load_sem.at[1]),
        pltpu.make_async_copy(wv, w.at[:, hd : 2 * hd], load_sem.at[2]),
        pltpu.make_async_copy(wlen_in, wlen, load_sem.at[3]),
        pltpu.make_async_copy(kwidth_in, kwidth, load_sem.at[4]),
        pltpu.make_async_copy(keep_in, keep, load_sem.at[5]),
    ]
    for cp in loads:
        cp.start()

    ring = {
        name: {"seq": at, "head": h}
        for name, at in (
            ("z+", y * n_z + lax.rem(z + 1, n_z)),
            ("z-", y * n_z + lax.rem(z + n_z - 1, n_z)),
            ("y+", lax.rem(y + 1, n_y) * n_z + z),
            ("y-", lax.rem(y + n_y - 1, n_y) * n_z + z),
        )
    }
    barrier = pltpu.get_barrier_semaphore()
    for dev in (right, left, partner, *ring.values()):
        pl.semaphore_signal(barrier, inc=1, device_id=dev, device_id_type=MESH)
    pl.semaphore_wait(barrier, 3 + len(ring))

    rounds = ["z"] * (n_z // 2 - 1) + ["y"] * (n_y // 2)

    def tell(r):
        for side in "+-":
            pl.semaphore_signal(met.at[r], inc=1, device_id=ring[rounds[r] + side], device_id_type=MESH)

    def meet(r):
        pl.semaphore_wait(met.at[r], 2)
        if r + 1 < len(rounds):
            tell(r + 1)

    tell(0)

    def part(k):
        return slice(k * rows, (k + 1) * rows)

    def send(source, slot, k, ssem, dev):
        return pltpu.make_async_remote_copy(
            src_ref=source, dst_ref=hbuf.at[slot, part(k)], send_sem=ssem,
            recv_sem=recv_sem.at[slot, k], device_id=dev, device_id_type=MESH,
        )

    started = []

    def go(cp):
        cp.start()
        started.append(cp)

    for k in range(CHUNKS):
        go(send(hid.at[part(k)], 1, k, own_send.at[0, k], right))
        go(send(hid.at[part(k)], 2, k, own_send.at[1, k], left))
    for k in range(CHUNKS):
        go(send(hid.at[part(k)], 4, k, d2d_own_send.at[k], partner))

    def landed(slot, k):
        send(hbuf.at[slot, part(k)], slot, k, own_send.at[0, 0], right).wait_recv()

    for b in range(nb):
        position = (s * tok + b * BLK + lax.broadcasted_iota(jnp.int32, (BLK, hd), 0)).astype(jnp.float32)
        angle = position * freq[0:1, :]
        lane = lax.broadcasted_iota(jnp.int32, (BLK, hd), 1)
        cos_t[b * BLK : (b + 1) * BLK, :] = jnp.cos(angle)
        sine = jnp.sin(angle)
        sin_t[b * BLK : (b + 1) * BLK, :] = jnp.where(lane < hd // 2, -sine, sine)
    for j in range(group):
        qs[j * window : (j + 1) * window, :] = q[:, j * hd : (j + 1) * hd]
    for cp in loads:
        cp.wait()

    def accumulate(slot, first, count, size, fresh=False):
        head = src[slot]
        offset = pl.multiple_of(head * feat, feat)

        def body(i, carry):
            at = pl.ds(pl.multiple_of(first + i * size, size), size)
            block = hbuf[slot, at, :].astype(jnp.float32)
            normed = (block * gain[0:1, pl.ds(offset, feat)]).astype(jnp.bfloat16)
            product = jnp.dot(normed, w[pl.ds(offset, feat), :], preferred_element_type=jnp.float32)
            square = block * block
            lanes = square[:, 0:128]
            for t in range(1, feat // 128):
                lanes = lanes + square[:, t * 128 : (t + 1) * 128]
            if fresh:
                acc[at, :] = product
                ssq[at, :] = lanes
            else:
                acc[at, :] += product
                ssq[at, :] += lanes
            return carry

        lax.fori_loop(0, count, body, 0)

    meet(0)
    accumulate(0, 0, nb, BLK, fresh=True)
    meet(1)
    for k in range(CHUNKS):
        landed(4, k)
    accumulate(4, 0, nb, BLK)

    per = BLK // rows
    for b in range(nb):
        for k in range(b * per, (b + 1) * per):
            landed(1, k)
            if k < half:
                go(send(hbuf.at[1, part(k)], 3, k, fwd_send.at[k], right))
            go(send(hbuf.at[1, part(k)], 5, k, d2d_send.at[0, k], partner))
            landed(2, k)
            if k >= half:
                go(send(hbuf.at[2, part(k)], 3, k, fwd_send.at[k], left))
            go(send(hbuf.at[2, part(k)], 6, k, d2d_send.at[1, k], partner))
        accumulate(1, b * BLK, 1, BLK)
        accumulate(2, b * BLK, 1, BLK)
        for k in range(b * per, (b + 1) * per):
            landed(5, k)
            landed(6, k)
        accumulate(5, b * BLK, 1, BLK)
        accumulate(6, b * BLK, 1, BLK)
        if 2 + b < len(rounds):
            meet(2 + b)

    lane_q = lax.broadcasted_iota(jnp.int32, (1, nq), 1)
    limit = total_tokens - window + lax.rem(lane_q, window)

    def scores_of(keys):
        return lax.dot_general(
            keys, qs[...], (((1,), (1,)), ((), ())), preferred_element_type=jnp.float32
        ) * hd ** (-0.5)

    def halo_copy(side, dev):
        return pltpu.make_async_remote_copy(
            src_ref=halo_send.at[side], dst_ref=halo_recv.at[side], send_sem=halo_ssem.at[side],
            recv_sem=halo_rsem.at[side], device_id=dev, device_id_type=MESH,
        )

    def finish(b):
        at = slice(b * BLK, (b + 1) * BLK)
        meansq = jnp.sum(ssq[at, :], axis=1, keepdims=True) / full_width
        inv = lax.rsqrt(meansq + 1e-05)
        kraw = acc[at, 0:hd] * inv
        vraw = acc[at, hd : 2 * hd] * inv
        keys = (kraw * cos_t[at, :] + pltpu.roll(kraw, hd // 2, 1) * sin_t[at, :]).astype(jnp.bfloat16)
        mag = jnp.sum(jnp.abs(vraw), axis=1, keepdims=True) / hd
        mag = jnp.broadcast_to(mag, (BLK, 128))
        vmag[at, :] = mag
        if b == 0:
            halo_send[0, 0] = keys[0:16, :].astype(jnp.float32)
            halo_send[0, 1] = mag[0:16, :]
            go(halo_copy(0, seq_prev))
        if b == nb - 1:
            halo_send[1, 0] = keys[BLK - 16 :, :].astype(jnp.float32)
            halo_send[1, 1] = mag[BLK - 16 :, :]
            go(halo_copy(1, seq_next))
        scores = scores_of(keys)
        token = s * tok + b * BLK + lax.broadcasted_iota(jnp.int32, (BLK, nq), 0)
        scores = jnp.where(token <= limit, scores, NEG)
        top = jnp.max(scores, axis=0, keepdims=True)
        expo = jnp.exp(scores - top)
        ex[at, :] = expo
        tot = jnp.sum(expo, axis=0, keepdims=True)
        for j in range(nq // 128):
            stat[b, j : j + 1, :] = top[:, j * 128 : (j + 1) * 128]
            stat[b, 4 + j : 5 + j, :] = tot[:, j * 128 : (j + 1) * 128]

    for k in range(half):
        landed(3, k)
        go(send(hbuf.at[3, part(k)], 7, k, d2d_send.at[2, k], partner))
        landed(3, half + k)
        go(send(hbuf.at[3, part(half + k)], 7, half + k, d2d_send.at[2, half + k], partner))
        if (k + 1) % per == 0:
            i = k // per
            for b in (i, nb // 2 + i):
                accumulate(3, b * BLK, 1, BLK)
                for m in range(b * per, (b + 1) * per):
                    landed(7, m)
                accumulate(7, b * BLK, 1, BLK)
                finish(b)

    merged = stat[0]
    for b in range(1, nb):
        other = stat[b]
        top = jnp.maximum(merged, other)
        scaled = pltpu.roll(jnp.exp(merged - top), 4, 0) * merged + pltpu.roll(jnp.exp(other - top), 4, 0) * other
        sub = lax.broadcasted_iota(jnp.int32, (8, 128), 0)
        merged = jnp.where(sub < 4, top, scaled)
    stat_recv[s] = merged

    def stat_copy(d):
        return pltpu.make_async_remote_copy(
            src_ref=stat_recv.at[s], dst_ref=stat_recv.at[s], send_sem=stat_ssem.at[d],
            recv_sem=stat_rsem.at[d], device_id={"seq": lax.rem(s + d, n_seq), "head": h}, device_id_type=MESH,
        )

    def blk_copy(d):
        return pltpu.make_async_remote_copy(
            src_ref=blk_recv.at[s], dst_ref=blk_recv.at[s], send_sem=blk_ssem.at[d],
            recv_sem=blk_rsem.at[d], device_id={"seq": lax.rem(s + d, n_seq), "head": h}, device_id_type=MESH,
        )

    def each_peer(act):
        def body(d, carry):
            act(d)
            return carry

        lax.fori_loop(1, n_seq, body, 0)

    each_peer(lambda d: stat_copy(d).start())

    halo_copy(0, seq_prev).wait_recv()
    halo_copy(1, seq_next).wait_recv()
    edge_keys = jnp.concatenate([halo_recv[0, 0], halo_recv[1, 0]], axis=0).astype(jnp.bfloat16)
    edge_scores = scores_of(edge_keys)
    edge_row = lax.broadcasted_iota(jnp.int32, (32, nq), 0)
    edge_token = jnp.where(edge_row < 16, (s + 1) * tok + edge_row, s * tok - 32 + edge_row)
    edge_ok = (edge_token >= 0) & (edge_token <= limit)
    edge_scores = jnp.where(edge_ok, edge_scores, NEG)
    edge_top = jnp.max(edge_scores, axis=0, keepdims=True)
    edge_expo = jnp.where(edge_ok, jnp.exp(edge_scores - edge_top), 0.0)
    for j in range(nq // 128):
        stat[nb, j : j + 1, :] = edge_top[:, j * 128 : (j + 1) * 128]

    each_peer(lambda d: stat_copy(d).wait_recv())
    everyone = stat_recv[...]
    row_top = jnp.max(everyone, axis=0)
    row_total = jnp.sum(pltpu.roll(jnp.exp(everyone - row_top[None]), 4, 1) * everyone, axis=0)
    row_total = pltpu.roll(row_total, 4, 0)
    sub8 = lax.broadcasted_iota(jnp.int32, (8, 128), 0)
    lane8 = lax.broadcasted_iota(jnp.int32, (8, 128), 1)
    wrow = lax.rem(lane8, window)
    used = (wrow >= window - wlen[0]) & (sub8 < 4)
    for b in range(nb + 1):
        factor = jnp.exp(stat[b] - row_top) / row_total
        gt[b] = jnp.where(used, factor, 0.0)

    def weighted(expo, b):
        total = expo[:, 0:128] * gt[b, 0:1, :]
        for j in range(1, nq // 128):
            total = total + expo[:, j * 128 : (j + 1) * 128] * gt[b, j : j + 1, :]
        return total

    ext[...] = jnp.zeros_like(ext)
    for b in range(nb):
        at = slice(b * BLK, (b + 1) * BLK)
        column = weighted(ex[at, :], b) * vmag[at, :]
        ext[b + 1 : b + 2, :] = jnp.sum(column.T, axis=0, keepdims=True)
    edge = weighted(edge_expo, nb)
    halo_p[...] = jnp.zeros_like(halo_p)
    halo_p[0:16, :] = edge[0:16, :] * halo_recv[0, 1]
    halo_p[BLK - 16 :, :] = edge[16:32, :] * halo_recv[1, 1]
    edge_row_sum = jnp.sum(halo_p[...].T, axis=0, keepdims=True)
    ext[0:1, :] = edge_row_sum
    ext[nb + 1 : nb + 2, :] = edge_row_sum

    here = ext[...]
    before = pltpu.roll(here, 1, 0)
    after = pltpu.roll(here, 7, 0)
    halfspan = (kwidth[0] - 1) // 2
    pooled = here
    for shift in range(1, (KERNEL_LIMIT - 1) // 2 + 1):
        ahead = pltpu.roll(jnp.where(lane8 >= shift, here, after), 128 - shift, 1)
        behind = pltpu.roll(jnp.where(lane8 < 128 - shift, here, before), shift, 1)
        wider = jnp.maximum(jnp.maximum(pooled, ahead), behind)
        pooled = jnp.where(shift <= halfspan, wider, pooled)
    sums = jnp.broadcast_to(jnp.sum(pooled, axis=1, keepdims=True), (8, 128))
    mine = (sub8 >= 1) & (sub8 <= nb)
    local = jnp.sum(jnp.where(mine & (lane8 == sub8 - 1), sums, 0.0), axis=0, keepdims=True)
    blocks_out[...] = local[:, 0:nb]
    placed = jnp.sum(jnp.where(mine & (lane8 == s * nb + sub8 - 1), sums, 0.0), axis=0, keepdims=True)
    blk_recv[s] = jnp.broadcast_to(placed, (8, 128))
    each_peer(lambda d: blk_copy(d).start())
    each_peer(lambda d: blk_copy(d).wait_recv())
    row = jnp.sum(blk_recv[...], axis=0)[0:1, :]
    by_lane = jnp.broadcast_to(row, (128, 128))
    by_sub = by_lane.T
    si = lax.broadcasted_iota(jnp.int32, (128, 128), 0)
    li = lax.broadcasted_iota(jnp.int32, (128, 128), 1)
    larger = (by_sub > by_lane) | ((by_sub == by_lane) & (si < li))
    rank = jnp.sum(larger.astype(jnp.float32), axis=0, keepdims=True)
    kept = jnp.sum(jnp.where(rank < keep[0].astype(jnp.float32), row, 0.0), axis=1, keepdims=True)
    frac_out[...] = kept / jnp.sum(row, axis=1, keepdims=True)

    for cp in started:
        cp.wait_send()
    each_peer(lambda d: stat_copy(d).wait_send())
    each_peer(lambda d: blk_copy(d).wait_send())


def solution(mesh):
    n_seq = mesh.shape["seq"]

    def local(hidden, gain, key_matrix, value_matrix, queries, window_len, kernel_width, kept_block_count):
        tok, feat = hidden.shape
        width, hd = key_matrix.shape
        nq = queries.shape[0] * queries.shape[1] // hd
        nb = tok // BLK
        freq = (500000.0 ** (-(np.arange(hd // 2) * 2.0) / hd)).astype(np.float32)
        freq = jnp.asarray(np.concatenate([freq, freq])[None, :])
        anyspace = pl.BlockSpec(memory_space=pl.ANY)
        vmem = pl.BlockSpec(memory_space=pltpu.VMEM)
        f32, bf16 = jnp.float32, jnp.bfloat16
        dma = pltpu.SemaphoreType.DMA
        blocks, frac = pl.pallas_call(
            functools.partial(kernel, n_seq),
            out_shape=(
                jax.ShapeDtypeStruct((1, nb), f32),
                jax.ShapeDtypeStruct((1, 1), f32),
            ),
            in_specs=[anyspace, vmem, anyspace, anyspace, vmem, anyspace, anyspace, anyspace, vmem],
            out_specs=(vmem, vmem),
            scratch_shapes=[
                pltpu.VMEM((8, tok, feat), bf16),
                pltpu.VMEM((width, 2 * hd), bf16),
                pltpu.VMEM((nq, hd), bf16),
                pltpu.VMEM((tok, hd), f32),
                pltpu.VMEM((tok, hd), f32),
                pltpu.VMEM((tok, 2 * hd), f32),
                pltpu.VMEM((tok, 128), f32),
                pltpu.VMEM((tok, 128), f32),
                pltpu.VMEM((tok, nq), f32),
                pltpu.VMEM((nb + 1, 8, 128), f32),
                pltpu.VMEM((nb + 1, 8, 128), f32),
                pltpu.VMEM((8, 128), f32),
                pltpu.VMEM((BLK, 128), f32),
                pltpu.VMEM((2, 2, 16, 128), f32),
                pltpu.VMEM((2, 2, 16, 128), f32),
                pltpu.VMEM((n_seq, 8, 128), f32),
                pltpu.VMEM((n_seq, 8, 128), f32),
                pltpu.SMEM((1,), jnp.int32),
                pltpu.SMEM((1,), jnp.int32),
                pltpu.SMEM((1,), jnp.int32),
                dma((6,)),
                dma((2, CHUNKS)),
                dma((CHUNKS,)),
                dma((CHUNKS,)),
                dma((3, CHUNKS)),
                dma((8, CHUNKS)),
                dma((2,)),
                dma((2,)),
                dma((n_seq,)),
                dma((n_seq,)),
                dma((n_seq,)),
                dma((n_seq,)),
                pltpu.SemaphoreType.REGULAR((N_Z // 2 - 1 + n_seq // N_Z // 2,)),
            ],
            compiler_params=pltpu.CompilerParams(
                collective_id=0, has_side_effects=True, vmem_limit_bytes=56 * 1024 * 1024
            ),
        )(
            hidden, gain.reshape(1, -1), key_matrix, value_matrix, queries,
            window_len, kernel_width, kept_block_count, freq,
        )
        return blocks, frac.reshape(1)

    return jax.shard_map(
        local,
        mesh=mesh,
        in_specs=(
            P("seq", "head"), P(), P(None, "head"), P(None, "head"), P(None, "head"),
            P("head"), P("head"), P("head"),
        ),
        out_specs=(P("head", "seq"), P("head")),
        check_vma=False,
    )
```

```python
import functools

import jax
import jax.numpy as jnp
import numpy as np
from jax import lax
from jax.experimental import pallas as pl
from jax.experimental.pallas import tpu as pltpu
from jax.sharding import PartitionSpec as P

MESH = pl.DeviceIdType.MESH
BLK = 128
KERNEL_LIMIT = 15
NX = 4
N_Z = 8
CHUNKS = 8
NEG = -1e30


def kernel(
    n_seq,
    hid, gain_in, wk, wv, q_in, counts_in, freq_in,
    out,
    hbuf, w, gain, q, freq, qs, qs_t, cos_t, sin_t, acc, ssq, vmag, ex, stat, gt, ext, halo_p,
    halo_send, halo_recv, stat_recv, blk_recv, counts,
    load_sem, own_send, fwd_send, d2d_own_send, d2d_send, recv_sem,
    halo_ssem, halo_rsem, stat_ssem, stat_rsem, blk_ssem, blk_rsem, met,
):
    tok = hid.shape[0]
    feat = hid.shape[1]
    hd = wk.shape[1]
    window = q_in.shape[0]
    group = q_in.shape[1] // hd
    nq = window * group
    nb = tok // BLK
    rows = tok // CHUNKS
    half = CHUNKS // 2
    full_width = gain_in.shape[1]
    total_tokens = tok * n_seq

    s = lax.axis_index("seq")
    h = lax.axis_index("head")
    x, c = h // 2, lax.rem(h, 2)
    n_z = N_Z
    n_y = n_seq // N_Z
    y, z = s // n_z, lax.rem(s, n_z)
    xr, xl, xo = lax.rem(x + 1, NX), lax.rem(x + 3, NX), lax.rem(x + 2, NX)
    right = {"seq": s, "head": xr * 2 + c}
    left = {"seq": s, "head": xl * 2 + c}
    partner = {"seq": s, "head": x * 2 + 1 - c}
    seq_next = {"seq": lax.rem(s + 1, n_seq), "head": h}
    seq_prev = {"seq": lax.rem(s + n_seq - 1, n_seq), "head": h}

    src = [x * 2 + c, xl * 2 + c, xr * 2 + c, xo * 2 + c]
    src += [x * 2 + 1 - c, xl * 2 + 1 - c, xr * 2 + 1 - c, xo * 2 + 1 - c]

    ring = {
        name: {"seq": at, "head": h}
        for name, at in (
            ("z+", y * n_z + lax.rem(z + 1, n_z)),
            ("z-", y * n_z + lax.rem(z + n_z - 1, n_z)),
            ("y+", lax.rem(y + 1, n_y) * n_z + z),
            ("y-", lax.rem(y + n_y - 1, n_y) * n_z + z),
        )
    }
    barrier = pltpu.get_barrier_semaphore()
    for dev in (right, left, partner, *ring.values()):
        pl.semaphore_signal(barrier, inc=1, device_id=dev, device_id_type=MESH)
    loads = [
        pltpu.make_async_copy(hid, hbuf.at[0], load_sem.at[0]),
        pltpu.make_async_copy(wk, w.at[:, 0:hd], load_sem.at[1]),
        pltpu.make_async_copy(wv, w.at[:, hd : 2 * hd], load_sem.at[2]),
        pltpu.make_async_copy(counts_in, counts, load_sem.at[3]),
        pltpu.make_async_copy(gain_in, gain, load_sem.at[4]),
        pltpu.make_async_copy(q_in, q, load_sem.at[5]),
        pltpu.make_async_copy(freq_in, freq, load_sem.at[6]),
    ]
    for cp in loads:
        cp.start()
    pl.semaphore_wait(barrier, 3 + len(ring))

    rounds = ["z"] * (n_z // 2 - 1) + ["y"] * (n_y // 2)

    def tell(r):
        for side in "+-":
            pl.semaphore_signal(met.at[r], inc=1, device_id=ring[rounds[r] + side], device_id_type=MESH)

    def meet(r):
        pl.semaphore_wait(met.at[r], 2)
        if r + 1 < len(rounds):
            tell(r + 1)

    tell(0)

    def part(k):
        return slice(k * rows, (k + 1) * rows)

    def send(source, slot, k, ssem, dev):
        return pltpu.make_async_remote_copy(
            src_ref=source, dst_ref=hbuf.at[slot, part(k)], send_sem=ssem,
            recv_sem=recv_sem.at[slot, k], device_id=dev, device_id_type=MESH,
        )

    started = []

    def go(cp):
        cp.start()
        started.append(cp)

    for k in range(CHUNKS):
        go(send(hid.at[part(k)], 1, k, own_send.at[0, k], right))
        go(send(hid.at[part(k)], 2, k, own_send.at[1, k], left))
    for k in range(CHUNKS):
        go(send(hid.at[part(k)], 4, k, d2d_own_send.at[k], partner))

    def landed(slot, k):
        send(hbuf.at[slot, part(k)], slot, k, own_send.at[0, 0], right).wait_recv()

    for cp in loads:
        cp.wait()
    for b in range(nb):
        position = (s * tok + b * BLK + lax.broadcasted_iota(jnp.int32, (BLK, hd), 0)).astype(jnp.float32)
        angle = position * freq[0:1, :]
        lane = lax.broadcasted_iota(jnp.int32, (BLK, hd), 1)
        cos_t[b * BLK : (b + 1) * BLK, :] = jnp.cos(angle)
        sine = jnp.sin(angle)
        sin_t[b * BLK : (b + 1) * BLK, :] = jnp.where(lane < hd // 2, -sine, sine)
    for j in range(group):
        qs[j * window : (j + 1) * window, :] = q[:, j * hd : (j + 1) * hd]
    qs_t[...] = qs[...].astype(jnp.float32).T.astype(jnp.bfloat16)

    def accumulate(slot, first, count, size, fresh=False):
        head = src[slot]
        offset = pl.multiple_of(head * feat, feat)

        def body(i, carry):
            at = pl.ds(pl.multiple_of(first + i * size, size), size)
            block = hbuf[slot, at, :].astype(jnp.float32)
            normed = (block * gain[0:1, pl.ds(offset, feat)]).astype(jnp.bfloat16)
            product = jnp.dot(normed, w[pl.ds(offset, feat), :], preferred_element_type=jnp.float32)
            square = block * block
            lanes = square[:, 0:128]
            for t in range(1, feat // 128):
                lanes = lanes + square[:, t * 128 : (t + 1) * 128]
            if fresh:
                acc[at, :] = product
                ssq[at, :] = lanes
            else:
                acc[at, :] += product
                ssq[at, :] += lanes
            return carry

        lax.fori_loop(0, count, body, 0)

    meet(0)
    accumulate(0, 0, nb, BLK, fresh=True)
    meet(1)
    for k in range(CHUNKS):
        landed(4, k)
    accumulate(4, 0, nb, BLK)

    per = BLK // rows
    for b in range(nb):
        for k in range(b * per, (b + 1) * per):
            landed(1, k)
            if k < half:
                go(send(hbuf.at[1, part(k)], 3, k, fwd_send.at[k], right))
            go(send(hbuf.at[1, part(k)], 5, k, d2d_send.at[0, k], partner))
            landed(2, k)
            if k >= half:
                go(send(hbuf.at[2, part(k)], 3, k, fwd_send.at[k], left))
            go(send(hbuf.at[2, part(k)], 6, k, d2d_send.at[1, k], partner))
        accumulate(1, b * BLK, 1, BLK)
        accumulate(2, b * BLK, 1, BLK)
        for k in range(b * per, (b + 1) * per):
            landed(5, k)
            landed(6, k)
        accumulate(5, b * BLK, 1, BLK)
        accumulate(6, b * BLK, 1, BLK)
        if 2 + b < len(rounds):
            meet(2 + b)

    lane_q = lax.broadcasted_iota(jnp.int32, (1, nq), 1)
    limit = total_tokens - window + lax.rem(lane_q, window)

    def scores_of(keys):
        return jnp.dot(keys, qs_t[...], preferred_element_type=jnp.float32) * hd ** (-0.5)

    def halo_copy(side, dev):
        return pltpu.make_async_remote_copy(
            src_ref=halo_send.at[side], dst_ref=halo_recv.at[side], send_sem=halo_ssem.at[side],
            recv_sem=halo_rsem.at[side], device_id=dev, device_id_type=MESH,
        )

    def finish(b):
        at = slice(b * BLK, (b + 1) * BLK)
        meansq = jnp.sum(ssq[at, :], axis=1, keepdims=True) / full_width
        inv = lax.rsqrt(meansq + 1e-05)
        kraw = acc[at, 0:hd] * inv
        vraw = acc[at, hd : 2 * hd] * inv
        keys = (kraw * cos_t[at, :] + pltpu.roll(kraw, hd // 2, 1) * sin_t[at, :]).astype(jnp.bfloat16)
        mag = jnp.sum(jnp.abs(vraw), axis=1, keepdims=True) / hd
        mag = jnp.broadcast_to(mag, (BLK, 128))
        vmag[at, :] = mag
        if b == 0:
            halo_send[0, 0] = keys[0:16, :].astype(jnp.float32)
            halo_send[0, 1] = mag[0:16, :]
            go(halo_copy(0, seq_prev))
        if b == nb - 1:
            halo_send[1, 0] = keys[BLK - 16 :, :].astype(jnp.float32)
            halo_send[1, 1] = mag[BLK - 16 :, :]
            go(halo_copy(1, seq_next))
        scores = scores_of(keys)
        token = s * tok + b * BLK + lax.broadcasted_iota(jnp.int32, (BLK, nq), 0)
        scores = jnp.where(token <= limit, scores, NEG)
        top = jnp.max(scores, axis=0, keepdims=True)
        expo = jnp.exp(scores - top)
        ex[at, :] = expo
        tot = jnp.sum(expo, axis=0, keepdims=True)
        for j in range(nq // 128):
            stat[b, j : j + 1, :] = top[:, j * 128 : (j + 1) * 128]
            stat[b, 4 + j : 5 + j, :] = tot[:, j * 128 : (j + 1) * 128]

    for k in range(half):
        landed(3, k)
        go(send(hbuf.at[3, part(k)], 7, k, d2d_send.at[2, k], partner))
        landed(3, half + k)
        go(send(hbuf.at[3, part(half + k)], 7, half + k, d2d_send.at[2, half + k], partner))
        if (k + 1) % per == 0:
            i = k // per
            for b in (i, nb // 2 + i):
                accumulate(3, b * BLK, 1, BLK)
                for m in range(b * per, (b + 1) * per):
                    landed(7, m)
                accumulate(7, b * BLK, 1, BLK)
                finish(b)

    merged = stat[0]
    for b in range(1, nb):
        other = stat[b]
        top = jnp.maximum(merged, other)
        scaled = pltpu.roll(jnp.exp(merged - top), 4, 0) * merged + pltpu.roll(jnp.exp(other - top), 4, 0) * other
        sub = lax.broadcasted_iota(jnp.int32, (8, 128), 0)
        merged = jnp.where(sub < 4, top, scaled)
    stat_recv[s] = merged

    def stat_copy(d):
        return pltpu.make_async_remote_copy(
            src_ref=stat_recv.at[s], dst_ref=stat_recv.at[s], send_sem=stat_ssem.at[d],
            recv_sem=stat_rsem.at[d], device_id={"seq": lax.rem(s + d, n_seq), "head": h}, device_id_type=MESH,
        )

    def blk_copy(d):
        return pltpu.make_async_remote_copy(
            src_ref=blk_recv.at[s], dst_ref=blk_recv.at[s], send_sem=blk_ssem.at[d],
            recv_sem=blk_rsem.at[d], device_id={"seq": lax.rem(s + d, n_seq), "head": h}, device_id_type=MESH,
        )

    def each_peer(act):
        def body(d, carry):
            act(d)
            return carry

        lax.fori_loop(1, n_seq, body, 0)

    each_peer(lambda d: stat_copy(d).start())

    halo_copy(0, seq_prev).wait_recv()
    halo_copy(1, seq_next).wait_recv()
    edge_keys = jnp.concatenate([halo_recv[0, 0], halo_recv[1, 0]], axis=0).astype(jnp.bfloat16)
    edge_scores = scores_of(edge_keys)
    edge_row = lax.broadcasted_iota(jnp.int32, (32, nq), 0)
    edge_token = jnp.where(edge_row < 16, (s + 1) * tok + edge_row, s * tok - 32 + edge_row)
    edge_ok = (edge_token >= 0) & (edge_token <= limit)
    edge_scores = jnp.where(edge_ok, edge_scores, NEG)
    edge_top = jnp.max(edge_scores, axis=0, keepdims=True)
    edge_expo = jnp.where(edge_ok, jnp.exp(edge_scores - edge_top), 0.0)
    for j in range(nq // 128):
        stat[nb, j : j + 1, :] = edge_top[:, j * 128 : (j + 1) * 128]

    each_peer(lambda d: stat_copy(d).wait_recv())
    everyone = stat_recv[...]
    row_top = jnp.max(everyone, axis=0)
    row_total = jnp.sum(pltpu.roll(jnp.exp(everyone - row_top[None]), 4, 1) * everyone, axis=0)
    row_total = pltpu.roll(row_total, 4, 0)
    sub8 = lax.broadcasted_iota(jnp.int32, (8, 128), 0)
    lane8 = lax.broadcasted_iota(jnp.int32, (8, 128), 1)
    wrow = lax.rem(lane8, window)
    used = (wrow >= window - counts[0:1, 0:1]) & (sub8 < 4)
    for b in range(nb + 1):
        factor = jnp.exp(stat[b] - row_top) / row_total
        gt[b] = jnp.where(used, factor, 0.0)

    def weighted(expo, b):
        total = expo[:, 0:128] * gt[b, 0:1, :]
        for j in range(1, nq // 128):
            total = total + expo[:, j * 128 : (j + 1) * 128] * gt[b, j : j + 1, :]
        return total

    ext[...] = jnp.zeros_like(ext)
    for b in range(nb):
        at = slice(b * BLK, (b + 1) * BLK)
        column = weighted(ex[at, :], b) * vmag[at, :]
        ext[b + 1 : b + 2, :] = jnp.sum(column.T, axis=0, keepdims=True)
    edge = weighted(edge_expo, nb)
    halo_p[...] = jnp.zeros_like(halo_p)
    halo_p[0:16, :] = edge[0:16, :] * halo_recv[0, 1]
    halo_p[BLK - 16 :, :] = edge[16:32, :] * halo_recv[1, 1]
    edge_row_sum = jnp.sum(halo_p[...].T, axis=0, keepdims=True)
    ext[0:1, :] = edge_row_sum
    ext[nb + 1 : nb + 2, :] = edge_row_sum

    here = ext[...]
    before = pltpu.roll(here, 1, 0)
    after = pltpu.roll(here, 7, 0)
    halfspan = lax.shift_right_logical(counts[0:1, 1:2] - 1, 1)
    pooled = here
    for shift in range(1, (KERNEL_LIMIT - 1) // 2 + 1):
        ahead = pltpu.roll(jnp.where(lane8 >= shift, here, after), 128 - shift, 1)
        behind = pltpu.roll(jnp.where(lane8 < 128 - shift, here, before), shift, 1)
        wider = jnp.maximum(jnp.maximum(pooled, ahead), behind)
        pooled = jnp.where(shift <= halfspan, wider, pooled)
    sums = jnp.broadcast_to(jnp.sum(pooled, axis=1, keepdims=True), (8, 128))
    mine = (sub8 >= 1) & (sub8 <= nb)
    local = jnp.sum(jnp.where(mine & (lane8 == sub8 - 1), sums, 0.0), axis=0, keepdims=True)
    placed = jnp.sum(jnp.where(mine & (lane8 == s * nb + sub8 - 1), sums, 0.0), axis=0, keepdims=True)
    blk_recv[s] = jnp.broadcast_to(placed, (8, 128))
    each_peer(lambda d: blk_copy(d).start())
    each_peer(lambda d: blk_copy(d).wait_recv())
    row = jnp.sum(blk_recv[...], axis=0)[0:1, :]
    by_lane = jnp.broadcast_to(row, (128, 128))
    by_sub = by_lane.T
    si = lax.broadcasted_iota(jnp.int32, (128, 128), 0)
    li = lax.broadcasted_iota(jnp.int32, (128, 128), 1)
    larger = (by_sub > by_lane) | ((by_sub == by_lane) & (si < li))
    rank = jnp.sum(larger.astype(jnp.float32), axis=0, keepdims=True)
    kept = jnp.sum(jnp.where(rank < counts[0:1, 2:3].astype(jnp.float32), row, 0.0), axis=1, keepdims=True)
    fraction = kept / jnp.sum(row, axis=1, keepdims=True)
    lane1 = lax.broadcasted_iota(jnp.int32, (1, 128), 1)
    out[...] = jnp.where(lane1 < nb, local, fraction)

    for cp in started:
        cp.wait_send()
    each_peer(lambda d: stat_copy(d).wait_send())
    each_peer(lambda d: blk_copy(d).wait_send())


def split_kernel(joined, blocks, frac):
    nb = blocks.shape[1]
    blocks[...] = joined[:, 0:nb]
    frac[...] = joined[:, nb : nb + 1]


def solution(mesh):
    n_seq = mesh.shape["seq"]

    def local(hidden, gain, key_matrix, value_matrix, queries, window_len, kernel_width, kept_block_count):
        tok, feat = hidden.shape
        width, hd = key_matrix.shape
        nq = queries.shape[0] * queries.shape[1] // hd
        nb = tok // BLK
        freq = (500000.0 ** (-(np.arange(hd // 2) * 2.0) / hd)).astype(np.float32)
        freq = jnp.asarray(np.concatenate([freq, freq])[None, :])
        anyspace = pl.BlockSpec(memory_space=pl.ANY)
        vmem = pl.BlockSpec(memory_space=pltpu.VMEM)
        f32, bf16 = jnp.float32, jnp.bfloat16
        dma = pltpu.SemaphoreType.DMA
        lane = lax.broadcasted_iota(jnp.int32, (1, 128), 1)
        row = lambda v: lax.broadcast_in_dim(v, (1, 128), (0,))
        counts = jnp.where(lane == 0, row(window_len), jnp.where(lane == 1, row(kernel_width), row(kept_block_count)))
        joined = pl.pallas_call(
            functools.partial(kernel, n_seq),
            out_shape=jax.ShapeDtypeStruct((1, 128), f32),
            in_specs=[anyspace] * 7,
            out_specs=vmem,
            scratch_shapes=[
                pltpu.VMEM((8, tok, feat), bf16),
                pltpu.VMEM((width, 2 * hd), bf16),
                pltpu.VMEM((1, width), f32),
                pltpu.VMEM(queries.shape, bf16),
                pltpu.VMEM((1, hd), f32),
                pltpu.VMEM((nq, hd), bf16),
                pltpu.VMEM((hd, nq), bf16),
                pltpu.VMEM((tok, hd), f32),
                pltpu.VMEM((tok, hd), f32),
                pltpu.VMEM((tok, 2 * hd), f32),
                pltpu.VMEM((tok, 128), f32),
                pltpu.VMEM((tok, 128), f32),
                pltpu.VMEM((tok, nq), f32),
                pltpu.VMEM((nb + 1, 8, 128), f32),
                pltpu.VMEM((nb + 1, 8, 128), f32),
                pltpu.VMEM((8, 128), f32),
                pltpu.VMEM((BLK, 128), f32),
                pltpu.VMEM((2, 2, 16, 128), f32),
                pltpu.VMEM((2, 2, 16, 128), f32),
                pltpu.VMEM((n_seq, 8, 128), f32),
                pltpu.VMEM((n_seq, 8, 128), f32),
                pltpu.VMEM((1, 128), jnp.int32),
                dma((7,)),
                dma((2, CHUNKS)),
                dma((CHUNKS,)),
                dma((CHUNKS,)),
                dma((3, CHUNKS)),
                dma((8, CHUNKS)),
                dma((2,)),
                dma((2,)),
                dma((n_seq,)),
                dma((n_seq,)),
                dma((n_seq,)),
                dma((n_seq,)),
                pltpu.SemaphoreType.REGULAR((N_Z // 2 - 1 + n_seq // N_Z // 2,)),
            ],
            compiler_params=pltpu.CompilerParams(
                collective_id=0, has_side_effects=True, vmem_limit_bytes=56 * 1024 * 1024
            ),
        )(
            hidden, gain.reshape(1, -1), key_matrix, value_matrix, queries,
            counts, freq,
        )
        blocks, frac = pl.pallas_call(
            split_kernel,
            out_shape=(jax.ShapeDtypeStruct((1, nb), f32), jax.ShapeDtypeStruct((1, 1), f32)),
            in_specs=[vmem],
            out_specs=(vmem, vmem),
        )(joined)
        return blocks, frac.reshape(1)

    return jax.shard_map(
        local,
        mesh=mesh,
        in_specs=(
            P("seq", "head"), P(), P(None, "head"), P(None, "head"), P(None, "head"),
            P("head"), P("head"), P("head"),
        ),
        out_specs=(P("head", "seq"), P("head")),
        check_vma=False,
    )
```

```python
import functools

import jax
import jax.numpy as jnp
import numpy as np
from jax import lax
from jax.experimental import pallas as pl
from jax.experimental.pallas import tpu as pltpu
from jax.sharding import PartitionSpec as P

MESH = pl.DeviceIdType.MESH
BLK = 128
KERNEL_LIMIT = 15
NX = 4
N_Z = 8
CHUNKS = 8
NEG = -1e30


def kernel(
    n_seq,
    hid, gain_in, wk, wv, q_in, counts_in, freq_in,
    out,
    hbuf, w, gain, q, freq, qs, qs_t, cos_t, sin_t, acc, ssq, vmag, ex, stat, gt, ext, halo_p,
    halo_send, halo_recv, stat_recv, blk_recv, counts,
    load_sem, own_send, fwd_send, d2d_own_send, d2d_send, recv_sem,
    halo_ssem, halo_rsem, stat_ssem, stat_rsem, blk_ssem, blk_rsem, met,
):
    tok = hid.shape[0]
    feat = hid.shape[1]
    hd = wk.shape[1]
    window = q_in.shape[0]
    group = q_in.shape[1] // hd
    nq = window * group
    nb = tok // BLK
    rows = tok // CHUNKS
    full_width = gain_in.shape[1]
    total_tokens = tok * n_seq

    s = lax.axis_index("seq")
    h = lax.axis_index("head")
    x, c = h // 2, lax.rem(h, 2)
    n_z = N_Z
    n_y = n_seq // N_Z
    y, z = s // n_z, lax.rem(s, n_z)
    xr, xl, xo = lax.rem(x + 1, NX), lax.rem(x + 3, NX), lax.rem(x + 2, NX)
    right = {"seq": s, "head": xr * 2 + c}
    left = {"seq": s, "head": xl * 2 + c}
    partner = {"seq": s, "head": x * 2 + 1 - c}
    seq_next = {"seq": lax.rem(s + 1, n_seq), "head": h}
    seq_prev = {"seq": lax.rem(s + n_seq - 1, n_seq), "head": h}

    src = [x * 2 + c, xl * 2 + c, xr * 2 + c, xo * 2 + c]
    src += [x * 2 + 1 - c, xl * 2 + 1 - c, xr * 2 + 1 - c, xo * 2 + 1 - c]

    ring = {
        name: {"seq": at, "head": h}
        for name, at in (
            ("z+", y * n_z + lax.rem(z + 1, n_z)),
            ("z-", y * n_z + lax.rem(z + n_z - 1, n_z)),
            ("y+", lax.rem(y + 1, n_y) * n_z + z),
            ("y-", lax.rem(y + n_y - 1, n_y) * n_z + z),
        )
    }
    barrier = pltpu.get_barrier_semaphore()
    for dev in (right, left, partner, *ring.values()):
        pl.semaphore_signal(barrier, inc=1, device_id=dev, device_id_type=MESH)
    loads = [
        pltpu.make_async_copy(hid, hbuf.at[0], load_sem.at[0]),
        pltpu.make_async_copy(wk, w.at[:, 0:hd], load_sem.at[1]),
        pltpu.make_async_copy(wv, w.at[:, hd : 2 * hd], load_sem.at[2]),
        pltpu.make_async_copy(counts_in, counts, load_sem.at[3]),
        pltpu.make_async_copy(gain_in, gain, load_sem.at[4]),
        pltpu.make_async_copy(q_in, q, load_sem.at[5]),
        pltpu.make_async_copy(freq_in, freq, load_sem.at[6]),
    ]
    for cp in loads:
        cp.start()
    pl.semaphore_wait(barrier, 3 + len(ring))

    rounds = ["z"] * (n_z // 2 - 1) + ["y"] * (n_y // 2)

    def tell(r):
        for side in "+-":
            pl.semaphore_signal(met.at[r], inc=1, device_id=ring[rounds[r] + side], device_id_type=MESH)

    def meet(r):
        pl.semaphore_wait(met.at[r], 2)
        if r + 1 < len(rounds):
            tell(r + 1)

    tell(0)

    def part(k):
        return slice(k * rows, (k + 1) * rows)

    def send(source, slot, k, ssem, dev):
        return pltpu.make_async_remote_copy(
            src_ref=source, dst_ref=hbuf.at[slot, part(k)], send_sem=ssem,
            recv_sem=recv_sem.at[slot, k], device_id=dev, device_id_type=MESH,
        )

    started = []

    def go(cp):
        cp.start()
        started.append(cp)

    for k in range(CHUNKS):
        go(send(hid.at[part(k)], 1, k, own_send.at[0, k], right))
        go(send(hid.at[part(k)], 2, k, own_send.at[1, k], left))
    for k in range(CHUNKS):
        go(send(hid.at[part(k)], 4, k, d2d_own_send.at[k], partner))

    def landed(slot, k):
        send(hbuf.at[slot, part(k)], slot, k, own_send.at[0, 0], right).wait_recv()

    for cp in loads:
        cp.wait()
    for b in range(nb):
        position = (s * tok + b * BLK + lax.broadcasted_iota(jnp.int32, (BLK, hd), 0)).astype(jnp.float32)
        angle = position * freq[0:1, :]
        lane = lax.broadcasted_iota(jnp.int32, (BLK, hd), 1)
        cos_t[b * BLK : (b + 1) * BLK, :] = jnp.cos(angle)
        sine = jnp.sin(angle)
        sin_t[b * BLK : (b + 1) * BLK, :] = jnp.where(lane < hd // 2, -sine, sine)
    for j in range(group):
        qs[j * window : (j + 1) * window, :] = q[:, j * hd : (j + 1) * hd]
    qs_t[...] = qs[...].astype(jnp.float32).T.astype(jnp.bfloat16)

    def accumulate(slot, first, count, size, fresh=False):
        head = src[slot]
        offset = pl.multiple_of(head * feat, feat)

        def body(i, carry):
            at = pl.ds(pl.multiple_of(first + i * size, size), size)
            block = hbuf[slot, at, :].astype(jnp.float32)
            normed = (block * gain[0:1, pl.ds(offset, feat)]).astype(jnp.bfloat16)
            product = jnp.dot(normed, w[pl.ds(offset, feat), :], preferred_element_type=jnp.float32)
            square = block * block
            lanes = square[:, 0:128]
            for t in range(1, feat // 128):
                lanes = lanes + square[:, t * 128 : (t + 1) * 128]
            if fresh:
                acc[at, :] = product
                ssq[at, :] = lanes
            else:
                acc[at, :] += product
                ssq[at, :] += lanes
            return carry

        lax.fori_loop(0, count, body, 0)

    meet(0)
    accumulate(0, 0, nb, BLK, fresh=True)
    meet(1)
    for k in range(CHUNKS):
        landed(4, k)
    accumulate(4, 0, nb, BLK)

    per = BLK // rows
    for b in range(nb):
        for k in range(b * per, (b + 1) * per):
            landed(1, k)
            if k % 2 == 0:
                go(send(hbuf.at[1, part(k)], 3, k, fwd_send.at[k], right))
            go(send(hbuf.at[1, part(k)], 5, k, d2d_send.at[0, k], partner))
            landed(2, k)
            if k % 2 == 1:
                go(send(hbuf.at[2, part(k)], 3, k, fwd_send.at[k], left))
            go(send(hbuf.at[2, part(k)], 6, k, d2d_send.at[1, k], partner))
        accumulate(1, b * BLK, 1, BLK)
        accumulate(2, b * BLK, 1, BLK)
        for k in range(b * per, (b + 1) * per):
            landed(5, k)
            landed(6, k)
        accumulate(5, b * BLK, 1, BLK)
        accumulate(6, b * BLK, 1, BLK)
        if 2 + b < len(rounds):
            meet(2 + b)

    lane_q = lax.broadcasted_iota(jnp.int32, (1, nq), 1)
    limit = total_tokens - window + lax.rem(lane_q, window)

    def scores_of(keys):
        return jnp.dot(keys, qs_t[...], preferred_element_type=jnp.float32) * hd ** (-0.5)

    def halo_copy(side, dev):
        return pltpu.make_async_remote_copy(
            src_ref=halo_send.at[side], dst_ref=halo_recv.at[side], send_sem=halo_ssem.at[side],
            recv_sem=halo_rsem.at[side], device_id=dev, device_id_type=MESH,
        )

    def finish(b):
        at = slice(b * BLK, (b + 1) * BLK)
        meansq = jnp.sum(ssq[at, :], axis=1, keepdims=True) / full_width
        inv = lax.rsqrt(meansq + 1e-05)
        kraw = acc[at, 0:hd] * inv
        vraw = acc[at, hd : 2 * hd] * inv
        keys = (kraw * cos_t[at, :] + pltpu.roll(kraw, hd // 2, 1) * sin_t[at, :]).astype(jnp.bfloat16)
        mag = jnp.sum(jnp.abs(vraw), axis=1, keepdims=True) / hd
        mag = jnp.broadcast_to(mag, (BLK, 128))
        vmag[at, :] = mag
        if b == 0:
            halo_send[0, 0] = keys[0:16, :].astype(jnp.float32)
            halo_send[0, 1] = mag[0:16, :]
            go(halo_copy(0, seq_prev))
        if b == nb - 1:
            halo_send[1, 0] = keys[BLK - 16 :, :].astype(jnp.float32)
            halo_send[1, 1] = mag[BLK - 16 :, :]
            go(halo_copy(1, seq_next))
        scores = scores_of(keys)
        token = s * tok + b * BLK + lax.broadcasted_iota(jnp.int32, (BLK, nq), 0)
        scores = jnp.where(token <= limit, scores, NEG)
        top = jnp.max(scores, axis=0, keepdims=True)
        expo = jnp.exp(scores - top)
        ex[at, :] = expo
        tot = jnp.sum(expo, axis=0, keepdims=True)
        for j in range(nq // 128):
            stat[b, j : j + 1, :] = top[:, j * 128 : (j + 1) * 128]
            stat[b, 4 + j : 5 + j, :] = tot[:, j * 128 : (j + 1) * 128]

    for b in range(nb):
        for k in range(b * per, (b + 1) * per):
            landed(3, k)
            go(send(hbuf.at[3, part(k)], 7, k, d2d_send.at[2, k], partner))
        accumulate(3, b * BLK, 1, BLK)
        for k in range(b * per, (b + 1) * per):
            landed(7, k)
        accumulate(7, b * BLK, 1, BLK)
        finish(b)

    merged = stat[0]
    for b in range(1, nb):
        other = stat[b]
        top = jnp.maximum(merged, other)
        scaled = pltpu.roll(jnp.exp(merged - top), 4, 0) * merged + pltpu.roll(jnp.exp(other - top), 4, 0) * other
        sub = lax.broadcasted_iota(jnp.int32, (8, 128), 0)
        merged = jnp.where(sub < 4, top, scaled)
    stat_recv[s] = merged

    def stat_copy(d):
        return pltpu.make_async_remote_copy(
            src_ref=stat_recv.at[s], dst_ref=stat_recv.at[s], send_sem=stat_ssem.at[d],
            recv_sem=stat_rsem.at[d], device_id={"seq": lax.rem(s + d, n_seq), "head": h}, device_id_type=MESH,
        )

    def blk_copy(d):
        return pltpu.make_async_remote_copy(
            src_ref=blk_recv.at[s], dst_ref=blk_recv.at[s], send_sem=blk_ssem.at[d],
            recv_sem=blk_rsem.at[d], device_id={"seq": lax.rem(s + d, n_seq), "head": h}, device_id_type=MESH,
        )

    def each_peer(act):
        def body(d, carry):
            act(d)
            return carry

        lax.fori_loop(1, n_seq, body, 0)

    each_peer(lambda d: stat_copy(d).start())

    halo_copy(0, seq_prev).wait_recv()
    halo_copy(1, seq_next).wait_recv()
    edge_keys = jnp.concatenate([halo_recv[0, 0], halo_recv[1, 0]], axis=0).astype(jnp.bfloat16)
    edge_scores = scores_of(edge_keys)
    edge_row = lax.broadcasted_iota(jnp.int32, (32, nq), 0)
    edge_token = jnp.where(edge_row < 16, (s + 1) * tok + edge_row, s * tok - 32 + edge_row)
    edge_ok = (edge_token >= 0) & (edge_token <= limit)
    edge_scores = jnp.where(edge_ok, edge_scores, NEG)
    edge_top = jnp.max(edge_scores, axis=0, keepdims=True)
    edge_expo = jnp.where(edge_ok, jnp.exp(edge_scores - edge_top), 0.0)
    for j in range(nq // 128):
        stat[nb, j : j + 1, :] = edge_top[:, j * 128 : (j + 1) * 128]

    each_peer(lambda d: stat_copy(d).wait_recv())
    everyone = stat_recv[...]
    row_top = jnp.max(everyone, axis=0)
    row_total = jnp.sum(pltpu.roll(jnp.exp(everyone - row_top[None]), 4, 1) * everyone, axis=0)
    row_total = pltpu.roll(row_total, 4, 0)
    sub8 = lax.broadcasted_iota(jnp.int32, (8, 128), 0)
    lane8 = lax.broadcasted_iota(jnp.int32, (8, 128), 1)
    wrow = lax.rem(lane8, window)
    used = (wrow >= window - counts[0:1, 0:1]) & (sub8 < 4)
    for b in range(nb + 1):
        factor = jnp.exp(stat[b] - row_top) / row_total
        gt[b] = jnp.where(used, factor, 0.0)

    def weighted(expo, b):
        total = expo[:, 0:128] * gt[b, 0:1, :]
        for j in range(1, nq // 128):
            total = total + expo[:, j * 128 : (j + 1) * 128] * gt[b, j : j + 1, :]
        return total

    ext[...] = jnp.zeros_like(ext)
    for b in range(nb):
        at = slice(b * BLK, (b + 1) * BLK)
        column = weighted(ex[at, :], b) * vmag[at, :]
        ext[b + 1 : b + 2, :] = jnp.sum(column.T, axis=0, keepdims=True)
    edge = weighted(edge_expo, nb)
    halo_p[...] = jnp.zeros_like(halo_p)
    halo_p[0:16, :] = edge[0:16, :] * halo_recv[0, 1]
    halo_p[BLK - 16 :, :] = edge[16:32, :] * halo_recv[1, 1]
    edge_row_sum = jnp.sum(halo_p[...].T, axis=0, keepdims=True)
    ext[0:1, :] = edge_row_sum
    ext[nb + 1 : nb + 2, :] = edge_row_sum

    here = ext[...]
    before = pltpu.roll(here, 1, 0)
    after = pltpu.roll(here, 7, 0)
    halfspan = lax.shift_right_logical(counts[0:1, 1:2] - 1, 1)
    pooled = here
    for shift in range(1, (KERNEL_LIMIT - 1) // 2 + 1):
        ahead = pltpu.roll(jnp.where(lane8 >= shift, here, after), 128 - shift, 1)
        behind = pltpu.roll(jnp.where(lane8 < 128 - shift, here, before), shift, 1)
        wider = jnp.maximum(jnp.maximum(pooled, ahead), behind)
        pooled = jnp.where(shift <= halfspan, wider, pooled)
    sums = jnp.broadcast_to(jnp.sum(pooled, axis=1, keepdims=True), (8, 128))
    mine = (sub8 >= 1) & (sub8 <= nb)
    local = jnp.sum(jnp.where(mine & (lane8 == sub8 - 1), sums, 0.0), axis=0, keepdims=True)
    placed = jnp.sum(jnp.where(mine & (lane8 == s * nb + sub8 - 1), sums, 0.0), axis=0, keepdims=True)
    blk_recv[s] = jnp.broadcast_to(placed, (8, 128))
    each_peer(lambda d: blk_copy(d).start())
    each_peer(lambda d: blk_copy(d).wait_recv())
    row = jnp.sum(blk_recv[...], axis=0)[0:1, :]
    by_lane = jnp.broadcast_to(row, (128, 128))
    by_sub = by_lane.T
    si = lax.broadcasted_iota(jnp.int32, (128, 128), 0)
    li = lax.broadcasted_iota(jnp.int32, (128, 128), 1)
    larger = (by_sub > by_lane) | ((by_sub == by_lane) & (si < li))
    rank = jnp.sum(larger.astype(jnp.float32), axis=0, keepdims=True)
    kept = jnp.sum(jnp.where(rank < counts[0:1, 2:3].astype(jnp.float32), row, 0.0), axis=1, keepdims=True)
    fraction = kept / jnp.sum(row, axis=1, keepdims=True)
    lane1 = lax.broadcasted_iota(jnp.int32, (1, 128), 1)
    out[...] = jnp.where(lane1 < nb, local, fraction)

    for cp in started:
        cp.wait_send()
    each_peer(lambda d: stat_copy(d).wait_send())
    each_peer(lambda d: blk_copy(d).wait_send())


def split_kernel(joined, blocks, frac):
    nb = blocks.shape[1]
    blocks[...] = joined[:, 0:nb]
    frac[...] = joined[:, nb : nb + 1]


def solution(mesh):
    n_seq = mesh.shape["seq"]

    def local(hidden, gain, key_matrix, value_matrix, queries, window_len, kernel_width, kept_block_count):
        tok, feat = hidden.shape
        width, hd = key_matrix.shape
        nq = queries.shape[0] * queries.shape[1] // hd
        nb = tok // BLK
        freq = (500000.0 ** (-(np.arange(hd // 2) * 2.0) / hd)).astype(np.float32)
        freq = jnp.asarray(np.concatenate([freq, freq])[None, :])
        anyspace = pl.BlockSpec(memory_space=pl.ANY)
        vmem = pl.BlockSpec(memory_space=pltpu.VMEM)
        f32, bf16 = jnp.float32, jnp.bfloat16
        dma = pltpu.SemaphoreType.DMA
        lane = lax.broadcasted_iota(jnp.int32, (1, 128), 1)
        row = lambda v: lax.broadcast_in_dim(v, (1, 128), (0,))
        counts = jnp.where(lane == 0, row(window_len), jnp.where(lane == 1, row(kernel_width), row(kept_block_count)))
        joined = pl.pallas_call(
            functools.partial(kernel, n_seq),
            out_shape=jax.ShapeDtypeStruct((1, 128), f32),
            in_specs=[anyspace] * 7,
            out_specs=vmem,
            scratch_shapes=[
                pltpu.VMEM((8, tok, feat), bf16),
                pltpu.VMEM((width, 2 * hd), bf16),
                pltpu.VMEM((1, width), f32),
                pltpu.VMEM(queries.shape, bf16),
                pltpu.VMEM((1, hd), f32),
                pltpu.VMEM((nq, hd), bf16),
                pltpu.VMEM((hd, nq), bf16),
                pltpu.VMEM((tok, hd), f32),
                pltpu.VMEM((tok, hd), f32),
                pltpu.VMEM((tok, 2 * hd), f32),
                pltpu.VMEM((tok, 128), f32),
                pltpu.VMEM((tok, 128), f32),
                pltpu.VMEM((tok, nq), f32),
                pltpu.VMEM((nb + 1, 8, 128), f32),
                pltpu.VMEM((nb + 1, 8, 128), f32),
                pltpu.VMEM((8, 128), f32),
                pltpu.VMEM((BLK, 128), f32),
                pltpu.VMEM((2, 2, 16, 128), f32),
                pltpu.VMEM((2, 2, 16, 128), f32),
                pltpu.VMEM((n_seq, 8, 128), f32),
                pltpu.VMEM((n_seq, 8, 128), f32),
                pltpu.VMEM((1, 128), jnp.int32),
                dma((7,)),
                dma((2, CHUNKS)),
                dma((CHUNKS,)),
                dma((CHUNKS,)),
                dma((3, CHUNKS)),
                dma((8, CHUNKS)),
                dma((2,)),
                dma((2,)),
                dma((n_seq,)),
                dma((n_seq,)),
                dma((n_seq,)),
                dma((n_seq,)),
                pltpu.SemaphoreType.REGULAR((N_Z // 2 - 1 + n_seq // N_Z // 2,)),
            ],
            compiler_params=pltpu.CompilerParams(
                collective_id=0, has_side_effects=True, vmem_limit_bytes=56 * 1024 * 1024
            ),
        )(
            hidden, gain.reshape(1, -1), key_matrix, value_matrix, queries,
            counts, freq,
        )
        blocks, frac = pl.pallas_call(
            split_kernel,
            out_shape=(jax.ShapeDtypeStruct((1, nb), f32), jax.ShapeDtypeStruct((1, 1), f32)),
            in_specs=[vmem],
            out_specs=(vmem, vmem),
        )(joined)
        return blocks, frac.reshape(1)

    return jax.shard_map(
        local,
        mesh=mesh,
        in_specs=(
            P("seq", "head"), P(), P(None, "head"), P(None, "head"), P(None, "head"),
            P("head"), P("head"), P("head"),
        ),
        out_specs=(P("head", "seq"), P("head")),
        check_vma=False,
    )
```

```python
import functools

import jax
import jax.numpy as jnp
import numpy as np
from jax import lax
from jax.experimental import pallas as pl
from jax.experimental.pallas import tpu as pltpu
from jax.sharding import PartitionSpec as P

MESH = pl.DeviceIdType.MESH
BLK = 128
KERNEL_LIMIT = 15
NX = 4
N_Z = 8
CHUNKS = 8
OWN = 2
NEG = -1e30


def kernel(
    n_seq,
    hid, gain_in, wk, wv, q_in, wlen, kwidth, keep, freq_in,
    out,
    hbuf, w, gain, q, freq, qs, qs_t, cos_t, sin_t, acc, ssq, vmag, ex, stat, gt, ext, halo_p,
    halo_send, halo_recv, stat_recv, blk_recv,
    load_sem, own_send, fwd_send, d2d_own_send, d2d_send, recv_sem,
    halo_ssem, halo_rsem, stat_ssem, stat_rsem, blk_ssem, blk_rsem, met,
):
    tok = hid.shape[0]
    feat = hid.shape[1]
    hd = wk.shape[1]
    window = q_in.shape[0]
    group = q_in.shape[1] // hd
    nq = window * group
    nb = tok // BLK
    rows = tok // CHUNKS
    full_width = gain_in.shape[1]
    total_tokens = tok * n_seq

    s = lax.axis_index("seq")
    h = lax.axis_index("head")
    x, c = h // 2, lax.rem(h, 2)
    n_z = N_Z
    n_y = n_seq // N_Z
    y, z = s // n_z, lax.rem(s, n_z)
    xr, xl, xo = lax.rem(x + 1, NX), lax.rem(x + 3, NX), lax.rem(x + 2, NX)
    right = {"seq": s, "head": xr * 2 + c}
    left = {"seq": s, "head": xl * 2 + c}
    partner = {"seq": s, "head": x * 2 + 1 - c}
    seq_next = {"seq": lax.rem(s + 1, n_seq), "head": h}
    seq_prev = {"seq": lax.rem(s + n_seq - 1, n_seq), "head": h}

    src = [x * 2 + c, xl * 2 + c, xr * 2 + c, xo * 2 + c]
    src += [x * 2 + 1 - c, xl * 2 + 1 - c, xr * 2 + 1 - c, xo * 2 + 1 - c]

    ring = {
        name: {"seq": at, "head": h}
        for name, at in (
            ("z+", y * n_z + lax.rem(z + 1, n_z)),
            ("z-", y * n_z + lax.rem(z + n_z - 1, n_z)),
            ("y+", lax.rem(y + 1, n_y) * n_z + z),
            ("y-", lax.rem(y + n_y - 1, n_y) * n_z + z),
        )
    }
    barrier = pltpu.get_barrier_semaphore()
    for dev in (right, left, partner, *ring.values()):
        pl.semaphore_signal(barrier, inc=1, device_id=dev, device_id_type=MESH)
    loads = [
        pltpu.make_async_copy(hid, hbuf.at[0], load_sem.at[0]),
        pltpu.make_async_copy(wk, w.at[:, 0:hd], load_sem.at[1]),
        pltpu.make_async_copy(wv, w.at[:, hd : 2 * hd], load_sem.at[2]),
        pltpu.make_async_copy(gain_in, gain, load_sem.at[3]),
        pltpu.make_async_copy(q_in, q, load_sem.at[4]),
        pltpu.make_async_copy(freq_in, freq, load_sem.at[5]),
    ]
    for cp in loads:
        cp.start()
    pl.semaphore_wait(barrier, 3 + len(ring))

    rounds = ["z"] * (n_z // 2 - 1) + ["y"] * (n_y // 2)

    def tell(r):
        for side in "+-":
            pl.semaphore_signal(met.at[r], inc=1, device_id=ring[rounds[r] + side], device_id_type=MESH)

    def meet(r):
        pl.semaphore_wait(met.at[r], 2)
        if r + 1 < len(rounds):
            tell(r + 1)

    tell(0)

    def part(k, n=CHUNKS):
        return slice(k * (tok // n), (k + 1) * (tok // n))

    def send(source, slot, k, ssem, dev, n=CHUNKS):
        return pltpu.make_async_remote_copy(
            src_ref=source, dst_ref=hbuf.at[slot, part(k, n)], send_sem=ssem,
            recv_sem=recv_sem.at[slot, k], device_id=dev, device_id_type=MESH,
        )

    started = []

    def go(cp):
        cp.start()
        started.append(cp)

    for k in range(OWN):
        go(send(hid.at[part(k, OWN)], 1, k, own_send.at[0, k], right, OWN))
        go(send(hid.at[part(k, OWN)], 2, k, own_send.at[1, k], left, OWN))
    for k in range(OWN):
        go(send(hid.at[part(k, OWN)], 4, k, d2d_own_send.at[k], partner, OWN))

    def landed(slot, k, n=CHUNKS):
        send(hbuf.at[slot, part(k, n)], slot, k, own_send.at[0, 0], right, n).wait_recv()

    for cp in loads:
        cp.wait()
    for b in range(nb):
        position = (s * tok + b * BLK + lax.broadcasted_iota(jnp.int32, (BLK, hd), 0)).astype(jnp.float32)
        angle = position * freq[0:1, :]
        lane = lax.broadcasted_iota(jnp.int32, (BLK, hd), 1)
        cos_t[b * BLK : (b + 1) * BLK, :] = jnp.cos(angle)
        sine = jnp.sin(angle)
        sin_t[b * BLK : (b + 1) * BLK, :] = jnp.where(lane < hd // 2, -sine, sine)
    for j in range(group):
        qs[j * window : (j + 1) * window, :] = q[:, j * hd : (j + 1) * hd]
    qs_t[...] = qs[...].astype(jnp.float32).T.astype(jnp.bfloat16)

    def accumulate(slot, first, count, size, fresh=False):
        head = src[slot]
        offset = pl.multiple_of(head * feat, feat)

        def body(i, carry):
            at = pl.ds(pl.multiple_of(first + i * size, size), size)
            block = hbuf[slot, at, :].astype(jnp.float32)
            normed = (block * gain[0:1, pl.ds(offset, feat)]).astype(jnp.bfloat16)
            product = jnp.dot(normed, w[pl.ds(offset, feat), :], preferred_element_type=jnp.float32)
            square = block * block
            lanes = square[:, 0:128]
            for t in range(1, feat // 128):
                lanes = lanes + square[:, t * 128 : (t + 1) * 128]
            if fresh:
                acc[at, :] = product
                ssq[at, :] = lanes
            else:
                acc[at, :] += product
                ssq[at, :] += lanes
            return carry

        lax.fori_loop(0, count, body, 0)

    meet(0)
    accumulate(0, 0, nb, BLK, fresh=True)
    meet(1)
    for k in range(OWN):
        landed(4, k, OWN)
    accumulate(4, 0, nb, BLK)

    per = BLK // rows
    for k in range(OWN):
        inside = range(k * CHUNKS // OWN, (k + 1) * CHUNKS // OWN)
        batches = nb // OWN
        landed(1, k, OWN)
        for m in inside:
            if m % 2 == 0:
                go(send(hbuf.at[1, part(m)], 3, m, fwd_send.at[m], right))
        go(send(hbuf.at[1, part(k, OWN)], 5, k, d2d_send.at[0, k], partner, OWN))
        landed(2, k, OWN)
        for m in inside:
            if m % 2 == 1:
                go(send(hbuf.at[2, part(m)], 3, m, fwd_send.at[m], left))
        go(send(hbuf.at[2, part(k, OWN)], 6, k, d2d_send.at[1, k], partner, OWN))
        accumulate(1, k * batches * BLK, batches, BLK)
        accumulate(2, k * batches * BLK, batches, BLK)
        landed(5, k, OWN)
        landed(6, k, OWN)
        accumulate(5, k * batches * BLK, batches, BLK)
        accumulate(6, k * batches * BLK, batches, BLK)
        meet(2 + k)
    for r in range(2 + OWN, len(rounds)):
        meet(r)

    lane_q = lax.broadcasted_iota(jnp.int32, (1, nq), 1)
    limit = total_tokens - window + lax.rem(lane_q, window)

    def scores_of(keys):
        return jnp.dot(keys, qs_t[...], preferred_element_type=jnp.float32) * hd ** (-0.5)

    def halo_copy(side, dev):
        return pltpu.make_async_remote_copy(
            src_ref=halo_send.at[side], dst_ref=halo_recv.at[side], send_sem=halo_ssem.at[side],
            recv_sem=halo_rsem.at[side], device_id=dev, device_id_type=MESH,
        )

    def finish(b):
        at = slice(b * BLK, (b + 1) * BLK)
        meansq = jnp.sum(ssq[at, :], axis=1, keepdims=True) / full_width
        inv = lax.rsqrt(meansq + 1e-05)
        kraw = acc[at, 0:hd] * inv
        vraw = acc[at, hd : 2 * hd] * inv
        keys = (kraw * cos_t[at, :] + pltpu.roll(kraw, hd // 2, 1) * sin_t[at, :]).astype(jnp.bfloat16)
        mag = jnp.sum(jnp.abs(vraw), axis=1, keepdims=True) / hd
        mag = jnp.broadcast_to(mag, (BLK, 128))
        vmag[at, :] = mag
        if b == 0:
            halo_send[0, 0] = keys[0:16, :].astype(jnp.float32)
            halo_send[0, 1] = mag[0:16, :]
            go(halo_copy(0, seq_prev))
        if b == nb - 1:
            halo_send[1, 0] = keys[BLK - 16 :, :].astype(jnp.float32)
            halo_send[1, 1] = mag[BLK - 16 :, :]
            go(halo_copy(1, seq_next))
        scores = scores_of(keys)
        token = s * tok + b * BLK + lax.broadcasted_iota(jnp.int32, (BLK, nq), 0)
        scores = jnp.where(token <= limit, scores, NEG)
        top = jnp.max(scores, axis=0, keepdims=True)
        expo = jnp.exp(scores - top)
        ex[at, :] = expo
        tot = jnp.sum(expo, axis=0, keepdims=True)
        for j in range(nq // 128):
            stat[b, j : j + 1, :] = top[:, j * 128 : (j + 1) * 128]
            stat[b, 4 + j : 5 + j, :] = tot[:, j * 128 : (j + 1) * 128]

    for b in range(nb):
        for k in range(b * per, (b + 1) * per):
            landed(3, k)
            go(send(hbuf.at[3, part(k)], 7, k, d2d_send.at[2, k], partner))
        accumulate(3, b * BLK, 1, BLK)
        for k in range(b * per, (b + 1) * per):
            landed(7, k)
        accumulate(7, b * BLK, 1, BLK)
        finish(b)

    merged = stat[0]
    for b in range(1, nb):
        other = stat[b]
        top = jnp.maximum(merged, other)
        scaled = pltpu.roll(jnp.exp(merged - top), 4, 0) * merged + pltpu.roll(jnp.exp(other - top), 4, 0) * other
        sub = lax.broadcasted_iota(jnp.int32, (8, 128), 0)
        merged = jnp.where(sub < 4, top, scaled)
    stat_recv[s] = merged

    def stat_copy(d):
        return pltpu.make_async_remote_copy(
            src_ref=stat_recv.at[s], dst_ref=stat_recv.at[s], send_sem=stat_ssem.at[d],
            recv_sem=stat_rsem.at[d], device_id={"seq": lax.rem(s + d, n_seq), "head": h}, device_id_type=MESH,
        )

    def blk_copy(d):
        return pltpu.make_async_remote_copy(
            src_ref=blk_recv.at[s, 0:1], dst_ref=blk_recv.at[s, 0:1], send_sem=blk_ssem.at[d],
            recv_sem=blk_rsem.at[d], device_id={"seq": lax.rem(s + d, n_seq), "head": h}, device_id_type=MESH,
        )

    def each_peer(act):
        def body(d, carry):
            act(d)
            return carry

        lax.fori_loop(1, n_seq, body, 0)

    each_peer(lambda d: stat_copy(d).start())

    halo_copy(0, seq_prev).wait_recv()
    halo_copy(1, seq_next).wait_recv()
    edge_keys = jnp.concatenate([halo_recv[0, 0], halo_recv[1, 0]], axis=0).astype(jnp.bfloat16)
    edge_scores = scores_of(edge_keys)
    edge_row = lax.broadcasted_iota(jnp.int32, (32, nq), 0)
    edge_token = jnp.where(edge_row < 16, (s + 1) * tok + edge_row, s * tok - 32 + edge_row)
    edge_ok = (edge_token >= 0) & (edge_token <= limit)
    edge_scores = jnp.where(edge_ok, edge_scores, NEG)
    edge_top = jnp.max(edge_scores, axis=0, keepdims=True)
    edge_expo = jnp.where(edge_ok, jnp.exp(edge_scores - edge_top), 0.0)
    for j in range(nq // 128):
        stat[nb, j : j + 1, :] = edge_top[:, j * 128 : (j + 1) * 128]

    each_peer(lambda d: stat_copy(d).wait_recv())
    everyone = stat_recv[...]
    row_top = jnp.max(everyone, axis=0)
    row_total = jnp.sum(pltpu.roll(jnp.exp(everyone - row_top[None]), 4, 1) * everyone, axis=0)
    row_total = pltpu.roll(row_total, 4, 0)
    sub8 = lax.broadcasted_iota(jnp.int32, (8, 128), 0)
    lane8 = lax.broadcasted_iota(jnp.int32, (8, 128), 1)
    wrow = lax.rem(lane8, window)
    used = (wrow >= window - wlen[0]) & (sub8 < 4)
    for b in range(nb + 1):
        factor = jnp.exp(stat[b] - row_top) / row_total
        gt[b] = jnp.where(used, factor, 0.0)

    def weighted(expo, b):
        total = expo[:, 0:128] * gt[b, 0:1, :]
        for j in range(1, nq // 128):
            total = total + expo[:, j * 128 : (j + 1) * 128] * gt[b, j : j + 1, :]
        return total

    ext[...] = jnp.zeros_like(ext)
    for b in range(nb):
        at = slice(b * BLK, (b + 1) * BLK)
        column = weighted(ex[at, :], b) * vmag[at, :]
        ext[b + 1 : b + 2, :] = jnp.sum(column.T, axis=0, keepdims=True)
    edge = weighted(edge_expo, nb)
    halo_p[...] = jnp.zeros_like(halo_p)
    halo_p[0:16, :] = edge[0:16, :] * halo_recv[0, 1]
    halo_p[BLK - 16 :, :] = edge[16:32, :] * halo_recv[1, 1]
    edge_row_sum = jnp.sum(halo_p[...].T, axis=0, keepdims=True)
    ext[0:1, :] = edge_row_sum
    ext[nb + 1 : nb + 2, :] = edge_row_sum

    here = ext[...]
    before = pltpu.roll(here, 1, 0)
    after = pltpu.roll(here, 7, 0)
    halfspan = (kwidth[0] - 1) // 2
    pooled = here
    for shift in range(1, (KERNEL_LIMIT - 1) // 2 + 1):
        ahead = pltpu.roll(jnp.where(lane8 >= shift, here, after), 128 - shift, 1)
        behind = pltpu.roll(jnp.where(lane8 < 128 - shift, here, before), shift, 1)
        wider = jnp.maximum(jnp.maximum(pooled, ahead), behind)
        pooled = jnp.where(shift <= halfspan, wider, pooled)
    sums = jnp.broadcast_to(jnp.sum(pooled, axis=1, keepdims=True), (8, 128))
    mine = (sub8 >= 1) & (sub8 <= nb)
    local = jnp.sum(jnp.where(mine & (lane8 == sub8 - 1), sums, 0.0), axis=0, keepdims=True)
    placed = jnp.sum(jnp.where(mine & (lane8 == s * nb + sub8 - 1), sums, 0.0), axis=0, keepdims=True)
    blk_recv[s, 0:1, :] = placed
    each_peer(lambda d: blk_copy(d).start())
    each_peer(lambda d: blk_copy(d).wait_recv())
    row = jnp.sum(blk_recv[:, 0:1, :], axis=0)
    by_lane = jnp.broadcast_to(row, (128, 128))
    by_sub = by_lane.T
    si = lax.broadcasted_iota(jnp.int32, (128, 128), 0)
    li = lax.broadcasted_iota(jnp.int32, (128, 128), 1)
    larger = (by_sub > by_lane) | ((by_sub == by_lane) & (si < li))
    rank = jnp.sum(larger.astype(jnp.float32), axis=0, keepdims=True)
    kept = jnp.sum(jnp.where(rank < keep[0].astype(jnp.float32), row, 0.0), axis=1, keepdims=True)
    fraction = kept / jnp.sum(row, axis=1, keepdims=True)
    lane1 = lax.broadcasted_iota(jnp.int32, (1, 128), 1)
    out[...] = jnp.where(lane1 < nb, local, fraction)

    for cp in started:
        cp.wait_send()
    each_peer(lambda d: stat_copy(d).wait_send())
    each_peer(lambda d: blk_copy(d).wait_send())


def split_kernel(joined, blocks, frac):
    nb = blocks.shape[1]
    blocks[...] = joined[:, 0:nb]
    frac[...] = joined[:, nb : nb + 1]


def solution(mesh):
    n_seq = mesh.shape["seq"]

    def local(hidden, gain, key_matrix, value_matrix, queries, window_len, kernel_width, kept_block_count):
        tok, feat = hidden.shape
        width, hd = key_matrix.shape
        nq = queries.shape[0] * queries.shape[1] // hd
        nb = tok // BLK
        freq = (500000.0 ** (-(np.arange(hd // 2) * 2.0) / hd)).astype(np.float32)
        freq = jnp.asarray(np.concatenate([freq, freq])[None, :])
        anyspace = pl.BlockSpec(memory_space=pl.ANY)
        vmem = pl.BlockSpec(memory_space=pltpu.VMEM)
        smem = pl.BlockSpec(memory_space=pltpu.SMEM)
        f32, bf16 = jnp.float32, jnp.bfloat16
        dma = pltpu.SemaphoreType.DMA
        joined = pl.pallas_call(
            functools.partial(kernel, n_seq),
            out_shape=jax.ShapeDtypeStruct((1, 128), f32),
            in_specs=[anyspace] * 5 + [smem] * 3 + [anyspace],
            out_specs=vmem,
            scratch_shapes=[
                pltpu.VMEM((8, tok, feat), bf16),
                pltpu.VMEM((width, 2 * hd), bf16),
                pltpu.VMEM((1, width), f32),
                pltpu.VMEM(queries.shape, bf16),
                pltpu.VMEM((1, hd), f32),
                pltpu.VMEM((nq, hd), bf16),
                pltpu.VMEM((hd, nq), bf16),
                pltpu.VMEM((tok, hd), f32),
                pltpu.VMEM((tok, hd), f32),
                pltpu.VMEM((tok, 2 * hd), f32),
                pltpu.VMEM((tok, 128), f32),
                pltpu.VMEM((tok, 128), f32),
                pltpu.VMEM((tok, nq), f32),
                pltpu.VMEM((nb + 1, 8, 128), f32),
                pltpu.VMEM((nb + 1, 8, 128), f32),
                pltpu.VMEM((8, 128), f32),
                pltpu.VMEM((BLK, 128), f32),
                pltpu.VMEM((2, 2, 16, 128), f32),
                pltpu.VMEM((2, 2, 16, 128), f32),
                pltpu.VMEM((n_seq, 8, 128), f32),
                pltpu.VMEM((n_seq, 8, 128), f32),
                dma((6,)),
                dma((2, CHUNKS)),
                dma((CHUNKS,)),
                dma((CHUNKS,)),
                dma((3, CHUNKS)),
                dma((8, CHUNKS)),
                dma((2,)),
                dma((2,)),
                dma((n_seq,)),
                dma((n_seq,)),
                dma((n_seq,)),
                dma((n_seq,)),
                pltpu.SemaphoreType.REGULAR((N_Z // 2 - 1 + n_seq // N_Z // 2,)),
            ],
            compiler_params=pltpu.CompilerParams(
                collective_id=0, has_side_effects=True, vmem_limit_bytes=56 * 1024 * 1024
            ),
        )(
            hidden, gain.reshape(1, -1), key_matrix, value_matrix, queries,
            window_len, kernel_width, kept_block_count, freq,
        )
        blocks, frac = pl.pallas_call(
            split_kernel,
            out_shape=(jax.ShapeDtypeStruct((1, nb), f32), jax.ShapeDtypeStruct((1, 1), f32)),
            in_specs=[vmem],
            out_specs=(vmem, vmem),
        )(joined)
        return blocks, frac.reshape(1)

    return jax.shard_map(
        local,
        mesh=mesh,
        in_specs=(
            P("seq", "head"), P(), P(None, "head"), P(None, "head"), P(None, "head"),
            P("head"), P("head"), P("head"),
        ),
        out_specs=(P("head", "seq"), P("head")),
        check_vma=False,
    )
```

```python
import functools

import jax
import jax.numpy as jnp
import numpy as np
from jax import lax
from jax.experimental import pallas as pl
from jax.experimental.pallas import tpu as pltpu
from jax.sharding import PartitionSpec as P

MESH = pl.DeviceIdType.MESH
BLK = 128
KERNEL_LIMIT = 15
NX = 4
N_Z = 8
CHUNKS = 8
OWN = 2
NEG = -1e30


def kernel(
    n_seq,
    hid, gain_in, wk, wv, q_in, wlen, kwidth, keep, freq_in,
    out,
    hbuf, w, gain, q, freq, qs, qs_t, cos_t, sin_t, acc, ssq, vmag, ex, stat, gt, ext, halo_p,
    halo_send, halo_recv, stat_recv, blk_recv,
    load_sem, own_send, fwd_send, d2d_own_send, d2d_send, recv_sem,
    halo_ssem, halo_rsem, stat_ssem, stat_rsem, blk_ssem, blk_rsem, met,
):
    tok = hid.shape[0]
    feat = hid.shape[1]
    hd = wk.shape[1]
    window = q_in.shape[0]
    group = q_in.shape[1] // hd
    nq = window * group
    nb = tok // BLK
    rows = tok // CHUNKS
    full_width = gain_in.shape[1]
    total_tokens = tok * n_seq

    s = lax.axis_index("seq")
    h = lax.axis_index("head")
    x, c = h // 2, lax.rem(h, 2)
    n_z = N_Z
    n_y = n_seq // N_Z
    y, z = s // n_z, lax.rem(s, n_z)
    xr, xl, xo = lax.rem(x + 1, NX), lax.rem(x + 3, NX), lax.rem(x + 2, NX)
    right = {"seq": s, "head": xr * 2 + c}
    left = {"seq": s, "head": xl * 2 + c}
    partner = {"seq": s, "head": x * 2 + 1 - c}
    seq_next = {"seq": lax.rem(s + 1, n_seq), "head": h}
    seq_prev = {"seq": lax.rem(s + n_seq - 1, n_seq), "head": h}

    src = [x * 2 + c, xl * 2 + c, xr * 2 + c, xo * 2 + c]
    src += [x * 2 + 1 - c, xl * 2 + 1 - c, xr * 2 + 1 - c, xo * 2 + 1 - c]

    ring = {
        name: {"seq": at, "head": h}
        for name, at in (
            ("z+", y * n_z + lax.rem(z + 1, n_z)),
            ("z-", y * n_z + lax.rem(z + n_z - 1, n_z)),
            ("y+", lax.rem(y + 1, n_y) * n_z + z),
            ("y-", lax.rem(y + n_y - 1, n_y) * n_z + z),
        )
    }
    barrier = pltpu.get_barrier_semaphore()
    for dev in (right, left, partner, *ring.values()):
        pl.semaphore_signal(barrier, inc=1, device_id=dev, device_id_type=MESH)
    loads = [
        pltpu.make_async_copy(hid, hbuf.at[0], load_sem.at[0]),
        pltpu.make_async_copy(wk, w.at[:, 0:hd], load_sem.at[1]),
        pltpu.make_async_copy(wv, w.at[:, hd : 2 * hd], load_sem.at[2]),
        pltpu.make_async_copy(gain_in, gain, load_sem.at[3]),
        pltpu.make_async_copy(q_in, q, load_sem.at[4]),
        pltpu.make_async_copy(freq_in, freq, load_sem.at[5]),
    ]
    for cp in loads:
        cp.start()
    pl.semaphore_wait(barrier, 3 + len(ring))

    rounds = ["z"] * (n_z // 2 - 1) + ["y"] * (n_y // 2)

    def tell(r):
        for side in "+-":
            pl.semaphore_signal(met.at[r], inc=1, device_id=ring[rounds[r] + side], device_id_type=MESH)

    def meet(r):
        pl.semaphore_wait(met.at[r], 2)
        if r + 1 < len(rounds):
            tell(r + 1)

    tell(0)

    def part(k, n=CHUNKS):
        return slice(k * (tok // n), (k + 1) * (tok // n))

    def send(source, slot, k, ssem, dev, n=CHUNKS):
        return pltpu.make_async_remote_copy(
            src_ref=source, dst_ref=hbuf.at[slot, part(k, n)], send_sem=ssem,
            recv_sem=recv_sem.at[slot, k], device_id=dev, device_id_type=MESH,
        )

    started = []

    def go(cp):
        cp.start()
        started.append(cp)

    for k in range(OWN):
        go(send(hid.at[part(k, OWN)], 1, k, own_send.at[0, k], right, OWN))
        go(send(hid.at[part(k, OWN)], 2, k, own_send.at[1, k], left, OWN))
    for k in range(OWN):
        go(send(hid.at[part(k, OWN)], 4, k, d2d_own_send.at[k], partner, OWN))

    def landed(slot, k, n=CHUNKS):
        send(hbuf.at[slot, part(k, n)], slot, k, own_send.at[0, 0], right, n).wait_recv()

    for cp in loads:
        cp.wait()
    for b in range(nb):
        position = (s * tok + b * BLK + lax.broadcasted_iota(jnp.int32, (BLK, hd), 0)).astype(jnp.float32)
        angle = position * freq[0:1, :]
        lane = lax.broadcasted_iota(jnp.int32, (BLK, hd), 1)
        cos_t[b * BLK : (b + 1) * BLK, :] = jnp.cos(angle)
        sine = jnp.sin(angle)
        sin_t[b * BLK : (b + 1) * BLK, :] = jnp.where(lane < hd // 2, -sine, sine)
    for j in range(group):
        qs[j * window : (j + 1) * window, :] = q[:, j * hd : (j + 1) * hd]
    qs_t[...] = qs[...].astype(jnp.float32).T.astype(jnp.bfloat16)

    def accumulate(slot, first, count, size, fresh=False):
        head = src[slot]
        offset = pl.multiple_of(head * feat, feat)

        def body(i, carry):
            at = pl.ds(pl.multiple_of(first + i * size, size), size)
            block = hbuf[slot, at, :].astype(jnp.float32)
            normed = (block * gain[0:1, pl.ds(offset, feat)]).astype(jnp.bfloat16)
            product = jnp.dot(normed, w[pl.ds(offset, feat), :], preferred_element_type=jnp.float32)
            square = block * block
            lanes = square[:, 0:128]
            for t in range(1, feat // 128):
                lanes = lanes + square[:, t * 128 : (t + 1) * 128]
            if fresh:
                acc[at, :] = product
                ssq[at, :] = lanes
            else:
                acc[at, :] += product
                ssq[at, :] += lanes
            return carry

        lax.fori_loop(0, count, body, 0)

    meet(0)
    accumulate(0, 0, nb, BLK, fresh=True)
    meet(1)
    for k in range(OWN):
        landed(4, k, OWN)
    accumulate(4, 0, nb, BLK)

    per = BLK // rows
    for k in range(OWN):
        inside = range(k * CHUNKS // OWN, (k + 1) * CHUNKS // OWN)
        batches = nb // OWN
        landed(1, k, OWN)
        for m in inside:
            if m % 2 == 0:
                go(send(hbuf.at[1, part(m)], 3, m, fwd_send.at[m], right))
        go(send(hbuf.at[1, part(k, OWN)], 5, k, d2d_send.at[0, k], partner, OWN))
        landed(2, k, OWN)
        for m in inside:
            if m % 2 == 1:
                go(send(hbuf.at[2, part(m)], 3, m, fwd_send.at[m], left))
        go(send(hbuf.at[2, part(k, OWN)], 6, k, d2d_send.at[1, k], partner, OWN))
        accumulate(1, k * batches * BLK, batches, BLK)
        accumulate(2, k * batches * BLK, batches, BLK)
        landed(5, k, OWN)
        landed(6, k, OWN)
        accumulate(5, k * batches * BLK, batches, BLK)
        accumulate(6, k * batches * BLK, batches, BLK)
        meet(2 + k)
    for r in range(2 + OWN, len(rounds)):
        meet(r)

    lane_q = lax.broadcasted_iota(jnp.int32, (1, nq), 1)
    limit = total_tokens - window + lax.rem(lane_q, window)

    def scores_of(keys):
        return jnp.dot(keys, qs_t[...], preferred_element_type=jnp.float32) * hd ** (-0.5)

    def halo_copy(side, dev):
        return pltpu.make_async_remote_copy(
            src_ref=halo_send.at[side], dst_ref=halo_recv.at[side], send_sem=halo_ssem.at[side],
            recv_sem=halo_rsem.at[side], device_id=dev, device_id_type=MESH,
        )

    def finish(b):
        at = slice(b * BLK, (b + 1) * BLK)
        meansq = jnp.sum(ssq[at, :], axis=1, keepdims=True) / full_width
        inv = lax.rsqrt(meansq + 1e-05)
        kraw = acc[at, 0:hd] * inv
        vraw = acc[at, hd : 2 * hd] * inv
        keys = (kraw * cos_t[at, :] + pltpu.roll(kraw, hd // 2, 1) * sin_t[at, :]).astype(jnp.bfloat16)
        mag = jnp.sum(jnp.abs(vraw), axis=1, keepdims=True) / hd
        mag = jnp.broadcast_to(mag, (BLK, 128))
        vmag[at, :] = mag
        if b == 0:
            halo_send[0, 0] = keys[0:16, :].astype(jnp.float32)
            halo_send[0, 1] = mag[0:16, :]
            go(halo_copy(0, seq_prev))
        if b == nb - 1:
            halo_send[1, 0] = keys[BLK - 16 :, :].astype(jnp.float32)
            halo_send[1, 1] = mag[BLK - 16 :, :]
            go(halo_copy(1, seq_next))
        scores = scores_of(keys)
        token = s * tok + b * BLK + lax.broadcasted_iota(jnp.int32, (BLK, nq), 0)
        scores = jnp.where(token <= limit, scores, NEG)
        top = jnp.max(scores, axis=0, keepdims=True)
        expo = jnp.exp(scores - top)
        ex[at, :] = expo
        tot = jnp.sum(expo, axis=0, keepdims=True)
        for j in range(nq // 128):
            stat[b, j : j + 1, :] = top[:, j * 128 : (j + 1) * 128]
            stat[b, 4 + j : 5 + j, :] = tot[:, j * 128 : (j + 1) * 128]

    for b in range(nb):
        for k in range(b * per, (b + 1) * per):
            landed(3, k)
            go(send(hbuf.at[3, part(k)], 7, k, d2d_send.at[2, k], partner))
        accumulate(3, b * BLK, 1, BLK)
        for k in range(b * per, (b + 1) * per):
            landed(7, k)
        accumulate(7, b * BLK, 1, BLK)
        finish(b)

    merged = stat[0]
    for b in range(1, nb):
        other = stat[b]
        top = jnp.maximum(merged, other)
        scaled = pltpu.roll(jnp.exp(merged - top), 4, 0) * merged + pltpu.roll(jnp.exp(other - top), 4, 0) * other
        sub = lax.broadcasted_iota(jnp.int32, (8, 128), 0)
        merged = jnp.where(sub < 4, top, scaled)
    stat_recv[s] = merged

    def peer(d):
        return {"seq": lax.rem(y + d // n_z, n_y) * n_z + lax.rem(z + d % n_z, n_z), "head": h}

    def stat_copy(d):
        return pltpu.make_async_remote_copy(
            src_ref=stat_recv.at[s], dst_ref=stat_recv.at[s], send_sem=stat_ssem.at[d],
            recv_sem=stat_rsem.at[d], device_id=peer(d), device_id_type=MESH,
        )

    def blk_copy(d):
        return pltpu.make_async_remote_copy(
            src_ref=blk_recv.at[s, 0:1], dst_ref=blk_recv.at[s, 0:1], send_sem=blk_ssem.at[d],
            recv_sem=blk_rsem.at[d], device_id=peer(d), device_id_type=MESH,
        )

    def distance(d):
        dy, dz = d // n_z, d % n_z
        return min(dy, n_y - dy) + min(dz, n_z - dz)

    peers = sorted(range(1, n_seq), key=lambda d: (-distance(d), d))

    def each_peer(act):
        for d in peers:
            act(d)

    each_peer(lambda d: stat_copy(d).start())

    halo_copy(0, seq_prev).wait_recv()
    halo_copy(1, seq_next).wait_recv()
    edge_keys = jnp.concatenate([halo_recv[0, 0], halo_recv[1, 0]], axis=0).astype(jnp.bfloat16)
    edge_scores = scores_of(edge_keys)
    edge_row = lax.broadcasted_iota(jnp.int32, (32, nq), 0)
    edge_token = jnp.where(edge_row < 16, (s + 1) * tok + edge_row, s * tok - 32 + edge_row)
    edge_ok = (edge_token >= 0) & (edge_token <= limit)
    edge_scores = jnp.where(edge_ok, edge_scores, NEG)
    edge_top = jnp.max(edge_scores, axis=0, keepdims=True)
    edge_expo = jnp.where(edge_ok, jnp.exp(edge_scores - edge_top), 0.0)
    for j in range(nq // 128):
        stat[nb, j : j + 1, :] = edge_top[:, j * 128 : (j + 1) * 128]

    each_peer(lambda d: stat_copy(d).wait_recv())
    everyone = stat_recv[...]
    row_top = jnp.max(everyone, axis=0)
    row_total = jnp.sum(pltpu.roll(jnp.exp(everyone - row_top[None]), 4, 1) * everyone, axis=0)
    row_total = pltpu.roll(row_total, 4, 0)
    sub8 = lax.broadcasted_iota(jnp.int32, (8, 128), 0)
    lane8 = lax.broadcasted_iota(jnp.int32, (8, 128), 1)
    wrow = lax.rem(lane8, window)
    used = (wrow >= window - wlen[0]) & (sub8 < 4)
    for b in range(nb + 1):
        factor = jnp.exp(stat[b] - row_top) / row_total
        gt[b] = jnp.where(used, factor, 0.0)

    def weighted(expo, b):
        total = expo[:, 0:128] * gt[b, 0:1, :]
        for j in range(1, nq // 128):
            total = total + expo[:, j * 128 : (j + 1) * 128] * gt[b, j : j + 1, :]
        return total

    ext[...] = jnp.zeros_like(ext)
    for b in range(nb):
        at = slice(b * BLK, (b + 1) * BLK)
        column = weighted(ex[at, :], b) * vmag[at, :]
        ext[b + 1 : b + 2, :] = jnp.sum(column.T, axis=0, keepdims=True)
    edge = weighted(edge_expo, nb)
    halo_p[...] = jnp.zeros_like(halo_p)
    halo_p[0:16, :] = edge[0:16, :] * halo_recv[0, 1]
    halo_p[BLK - 16 :, :] = edge[16:32, :] * halo_recv[1, 1]
    edge_row_sum = jnp.sum(halo_p[...].T, axis=0, keepdims=True)
    ext[0:1, :] = edge_row_sum
    ext[nb + 1 : nb + 2, :] = edge_row_sum

    here = ext[...]
    before = pltpu.roll(here, 1, 0)
    after = pltpu.roll(here, 7, 0)
    halfspan = (kwidth[0] - 1) // 2
    pooled = here
    for shift in range(1, (KERNEL_LIMIT - 1) // 2 + 1):
        ahead = pltpu.roll(jnp.where(lane8 >= shift, here, after), 128 - shift, 1)
        behind = pltpu.roll(jnp.where(lane8 < 128 - shift, here, before), shift, 1)
        wider = jnp.maximum(jnp.maximum(pooled, ahead), behind)
        pooled = jnp.where(shift <= halfspan, wider, pooled)
    sums = jnp.broadcast_to(jnp.sum(pooled, axis=1, keepdims=True), (8, 128))
    mine = (sub8 >= 1) & (sub8 <= nb)
    local = jnp.sum(jnp.where(mine & (lane8 == sub8 - 1), sums, 0.0), axis=0, keepdims=True)
    placed = jnp.sum(jnp.where(mine & (lane8 == s * nb + sub8 - 1), sums, 0.0), axis=0, keepdims=True)
    blk_recv[s, 0:1, :] = placed
    each_peer(lambda d: blk_copy(d).start())
    each_peer(lambda d: blk_copy(d).wait_recv())
    row = jnp.sum(blk_recv[:, 0:1, :], axis=0)
    by_lane = jnp.broadcast_to(row, (128, 128))
    by_sub = by_lane.T
    si = lax.broadcasted_iota(jnp.int32, (128, 128), 0)
    li = lax.broadcasted_iota(jnp.int32, (128, 128), 1)
    larger = (by_sub > by_lane) | ((by_sub == by_lane) & (si < li))
    rank = jnp.sum(larger.astype(jnp.float32), axis=0, keepdims=True)
    kept = jnp.sum(jnp.where(rank < keep[0].astype(jnp.float32), row, 0.0), axis=1, keepdims=True)
    fraction = kept / jnp.sum(row, axis=1, keepdims=True)
    lane1 = lax.broadcasted_iota(jnp.int32, (1, 128), 1)
    out[...] = jnp.where(lane1 < nb, local, fraction)

    for cp in started:
        cp.wait_send()
    each_peer(lambda d: stat_copy(d).wait_send())
    each_peer(lambda d: blk_copy(d).wait_send())


def split_kernel(joined, blocks, frac):
    nb = blocks.shape[1]
    blocks[...] = joined[:, 0:nb]
    frac[...] = joined[:, nb : nb + 1]


def solution(mesh):
    n_seq = mesh.shape["seq"]

    def local(hidden, gain, key_matrix, value_matrix, queries, window_len, kernel_width, kept_block_count):
        tok, feat = hidden.shape
        width, hd = key_matrix.shape
        nq = queries.shape[0] * queries.shape[1] // hd
        nb = tok // BLK
        freq = (500000.0 ** (-(np.arange(hd // 2) * 2.0) / hd)).astype(np.float32)
        freq = jnp.asarray(np.concatenate([freq, freq])[None, :])
        anyspace = pl.BlockSpec(memory_space=pl.ANY)
        vmem = pl.BlockSpec(memory_space=pltpu.VMEM)
        smem = pl.BlockSpec(memory_space=pltpu.SMEM)
        f32, bf16 = jnp.float32, jnp.bfloat16
        dma = pltpu.SemaphoreType.DMA
        joined = pl.pallas_call(
            functools.partial(kernel, n_seq),
            out_shape=jax.ShapeDtypeStruct((1, 128), f32),
            in_specs=[anyspace] * 5 + [smem] * 3 + [anyspace],
            out_specs=vmem,
            scratch_shapes=[
                pltpu.VMEM((8, tok, feat), bf16),
                pltpu.VMEM((width, 2 * hd), bf16),
                pltpu.VMEM((1, width), f32),
                pltpu.VMEM(queries.shape, bf16),
                pltpu.VMEM((1, hd), f32),
                pltpu.VMEM((nq, hd), bf16),
                pltpu.VMEM((hd, nq), bf16),
                pltpu.VMEM((tok, hd), f32),
                pltpu.VMEM((tok, hd), f32),
                pltpu.VMEM((tok, 2 * hd), f32),
                pltpu.VMEM((tok, 128), f32),
                pltpu.VMEM((tok, 128), f32),
                pltpu.VMEM((tok, nq), f32),
                pltpu.VMEM((nb + 1, 8, 128), f32),
                pltpu.VMEM((nb + 1, 8, 128), f32),
                pltpu.VMEM((8, 128), f32),
                pltpu.VMEM((BLK, 128), f32),
                pltpu.VMEM((2, 2, 16, 128), f32),
                pltpu.VMEM((2, 2, 16, 128), f32),
                pltpu.VMEM((n_seq, 8, 128), f32),
                pltpu.VMEM((n_seq, 8, 128), f32),
                dma((6,)),
                dma((2, CHUNKS)),
                dma((CHUNKS,)),
                dma((CHUNKS,)),
                dma((3, CHUNKS)),
                dma((8, CHUNKS)),
                dma((2,)),
                dma((2,)),
                dma((n_seq,)),
                dma((n_seq,)),
                dma((n_seq,)),
                dma((n_seq,)),
                pltpu.SemaphoreType.REGULAR((N_Z // 2 - 1 + n_seq // N_Z // 2,)),
            ],
            compiler_params=pltpu.CompilerParams(
                collective_id=0, has_side_effects=True, vmem_limit_bytes=56 * 1024 * 1024
            ),
        )(
            hidden, gain.reshape(1, -1), key_matrix, value_matrix, queries,
            window_len, kernel_width, kept_block_count, freq,
        )
        blocks, frac = pl.pallas_call(
            split_kernel,
            out_shape=(jax.ShapeDtypeStruct((1, nb), f32), jax.ShapeDtypeStruct((1, 1), f32)),
            in_specs=[vmem],
            out_specs=(vmem, vmem),
        )(joined)
        return blocks, frac.reshape(1)

    return jax.shard_map(
        local,
        mesh=mesh,
        in_specs=(
            P("seq", "head"), P(), P(None, "head"), P(None, "head"), P(None, "head"),
            P("head"), P("head"), P("head"),
        ),
        out_specs=(P("head", "seq"), P("head")),
        check_vma=False,
    )
```

```python
import functools

import jax
import jax.numpy as jnp
import numpy as np
from jax import lax
from jax.experimental import pallas as pl
from jax.experimental.pallas import tpu as pltpu
from jax.sharding import PartitionSpec as P

MESH = pl.DeviceIdType.MESH
BLK = 128
KERNEL_LIMIT = 15
NX = 4
N_Z = 8
CHUNKS = 8
OWN = 2
NEG = -1e30


def kernel(
    n_seq,
    hid, gain_in, wk, wv, q_in, wlen, kwidth, keep, freq_in,
    out,
    hbuf, w, gain, q, freq, qs, qs_t, cos_t, sin_t, acc, ssq, vmag, ex, stat, gt, ext, halo_p,
    halo_send, halo_recv, stat_recv, blk_recv,
    load_sem, own_send, fwd_send, d2d_own_send, d2d_send, recv_sem,
    halo_ssem, halo_rsem, stat_ssem, stat_rsem, blk_ssem, blk_rsem, met,
):
    tok = hid.shape[0]
    feat = hid.shape[1]
    hd = wk.shape[1]
    window = q_in.shape[0]
    group = q_in.shape[1] // hd
    nq = window * group
    nb = tok // BLK
    rows = tok // CHUNKS
    full_width = gain_in.shape[1]
    total_tokens = tok * n_seq

    s = lax.axis_index("seq")
    h = lax.axis_index("head")
    x, c = h // 2, lax.rem(h, 2)
    n_z = N_Z
    n_y = n_seq // N_Z
    y, z = s // n_z, lax.rem(s, n_z)
    xr, xl, xo = lax.rem(x + 1, NX), lax.rem(x + 3, NX), lax.rem(x + 2, NX)
    right = {"seq": s, "head": xr * 2 + c}
    left = {"seq": s, "head": xl * 2 + c}
    partner = {"seq": s, "head": x * 2 + 1 - c}
    seq_next = {"seq": lax.rem(s + 1, n_seq), "head": h}
    seq_prev = {"seq": lax.rem(s + n_seq - 1, n_seq), "head": h}

    src = [x * 2 + c, xl * 2 + c, xr * 2 + c, xo * 2 + c]
    src += [x * 2 + 1 - c, xl * 2 + 1 - c, xr * 2 + 1 - c, xo * 2 + 1 - c]

    ring = {
        name: {"seq": at, "head": h}
        for name, at in (
            ("z+", y * n_z + lax.rem(z + 1, n_z)),
            ("z-", y * n_z + lax.rem(z + n_z - 1, n_z)),
            ("y+", lax.rem(y + 1, n_y) * n_z + z),
            ("y-", lax.rem(y + n_y - 1, n_y) * n_z + z),
        )
    }
    barrier = pltpu.get_barrier_semaphore()
    for dev in (right, left, partner, *ring.values()):
        pl.semaphore_signal(barrier, inc=1, device_id=dev, device_id_type=MESH)
    loads = [
        pltpu.make_async_copy(hid, hbuf.at[0], load_sem.at[0]),
        pltpu.make_async_copy(wk, w.at[:, 0:hd], load_sem.at[1]),
        pltpu.make_async_copy(wv, w.at[:, hd : 2 * hd], load_sem.at[2]),
        pltpu.make_async_copy(gain_in, gain, load_sem.at[3]),
        pltpu.make_async_copy(q_in, q, load_sem.at[4]),
        pltpu.make_async_copy(freq_in, freq, load_sem.at[5]),
    ]
    pl.semaphore_wait(barrier, 3 + len(ring))

    rounds = ["z"] * (n_z // 2 - 1) + ["y"] * (n_y // 2)

    def tell(r):
        for side in "+-":
            pl.semaphore_signal(met.at[r], inc=1, device_id=ring[rounds[r] + side], device_id_type=MESH)

    def meet(r):
        pl.semaphore_wait(met.at[r], 2)
        if r + 1 < len(rounds):
            tell(r + 1)

    def part(k, n=CHUNKS):
        return slice(k * (tok // n), (k + 1) * (tok // n))

    def send(source, slot, k, ssem, dev, n=CHUNKS):
        return pltpu.make_async_remote_copy(
            src_ref=source, dst_ref=hbuf.at[slot, part(k, n)], send_sem=ssem,
            recv_sem=recv_sem.at[slot, k], device_id=dev, device_id_type=MESH,
        )

    started = []

    def go(cp):
        cp.start()
        started.append(cp)

    for k in range(OWN):
        go(send(hid.at[part(k, OWN)], 1, k, own_send.at[0, k], right, OWN))
        go(send(hid.at[part(k, OWN)], 2, k, own_send.at[1, k], left, OWN))
    for k in range(OWN):
        go(send(hid.at[part(k, OWN)], 4, k, d2d_own_send.at[k], partner, OWN))

    for cp in loads:
        cp.start()
    tell(0)

    def landed(slot, k, n=CHUNKS):
        send(hbuf.at[slot, part(k, n)], slot, k, own_send.at[0, 0], right, n).wait_recv()

    for cp in loads:
        cp.wait()
    for b in range(nb):
        position = (s * tok + b * BLK + lax.broadcasted_iota(jnp.int32, (BLK, hd), 0)).astype(jnp.float32)
        angle = position * freq[0:1, :]
        lane = lax.broadcasted_iota(jnp.int32, (BLK, hd), 1)
        cos_t[b * BLK : (b + 1) * BLK, :] = jnp.cos(angle)
        sine = jnp.sin(angle)
        sin_t[b * BLK : (b + 1) * BLK, :] = jnp.where(lane < hd // 2, -sine, sine)
    for j in range(group):
        qs[j * window : (j + 1) * window, :] = q[:, j * hd : (j + 1) * hd]
    qs_t[...] = qs[...].astype(jnp.float32).T.astype(jnp.bfloat16)

    def accumulate(slot, first, count, size, fresh=False):
        head = src[slot]
        offset = pl.multiple_of(head * feat, feat)

        def body(i, carry):
            at = pl.ds(pl.multiple_of(first + i * size, size), size)
            block = hbuf[slot, at, :].astype(jnp.float32)
            normed = (block * gain[0:1, pl.ds(offset, feat)]).astype(jnp.bfloat16)
            product = jnp.dot(normed, w[pl.ds(offset, feat), :], preferred_element_type=jnp.float32)
            square = block * block
            lanes = square[:, 0:128]
            for t in range(1, feat // 128):
                lanes = lanes + square[:, t * 128 : (t + 1) * 128]
            if fresh:
                acc[at, :] = product
                ssq[at, :] = lanes
            else:
                acc[at, :] += product
                ssq[at, :] += lanes
            return carry

        lax.fori_loop(0, count, body, 0)

    meet(0)
    accumulate(0, 0, nb, BLK, fresh=True)
    meet(1)
    for k in range(OWN):
        landed(4, k, OWN)
    accumulate(4, 0, nb, BLK)

    per = BLK // rows
    for k in range(OWN):
        inside = range(k * CHUNKS // OWN, (k + 1) * CHUNKS // OWN)
        batches = nb // OWN
        landed(1, k, OWN)
        for m in inside:
            if m % 2 == 0:
                go(send(hbuf.at[1, part(m)], 3, m, fwd_send.at[m], right))
        go(send(hbuf.at[1, part(k, OWN)], 5, k, d2d_send.at[0, k], partner, OWN))
        landed(2, k, OWN)
        for m in inside:
            if m % 2 == 1:
                go(send(hbuf.at[2, part(m)], 3, m, fwd_send.at[m], left))
        go(send(hbuf.at[2, part(k, OWN)], 6, k, d2d_send.at[1, k], partner, OWN))
        accumulate(1, k * batches * BLK, batches, BLK)
        accumulate(2, k * batches * BLK, batches, BLK)
        landed(5, k, OWN)
        landed(6, k, OWN)
        accumulate(5, k * batches * BLK, batches, BLK)
        accumulate(6, k * batches * BLK, batches, BLK)
        meet(2 + k)
    for r in range(2 + OWN, len(rounds)):
        meet(r)

    lane_q = lax.broadcasted_iota(jnp.int32, (1, nq), 1)
    limit = total_tokens - window + lax.rem(lane_q, window)

    def scores_of(keys):
        return jnp.dot(keys, qs_t[...], preferred_element_type=jnp.float32) * hd ** (-0.5)

    def halo_copy(side, dev):
        return pltpu.make_async_remote_copy(
            src_ref=halo_send.at[side], dst_ref=halo_recv.at[side], send_sem=halo_ssem.at[side],
            recv_sem=halo_rsem.at[side], device_id=dev, device_id_type=MESH,
        )

    def finish(b):
        at = slice(b * BLK, (b + 1) * BLK)
        meansq = jnp.sum(ssq[at, :], axis=1, keepdims=True) / full_width
        inv = lax.rsqrt(meansq + 1e-05)
        kraw = acc[at, 0:hd] * inv
        vraw = acc[at, hd : 2 * hd] * inv
        keys = (kraw * cos_t[at, :] + pltpu.roll(kraw, hd // 2, 1) * sin_t[at, :]).astype(jnp.bfloat16)
        mag = jnp.sum(jnp.abs(vraw), axis=1, keepdims=True) / hd
        mag = jnp.broadcast_to(mag, (BLK, 128))
        vmag[at, :] = mag
        if b == 0:
            halo_send[0, 0] = keys[0:16, :].astype(jnp.float32)
            halo_send[0, 1] = mag[0:16, :]
            go(halo_copy(0, seq_prev))
        if b == nb - 1:
            halo_send[1, 0] = keys[BLK - 16 :, :].astype(jnp.float32)
            halo_send[1, 1] = mag[BLK - 16 :, :]
            go(halo_copy(1, seq_next))
        scores = scores_of(keys)
        token = s * tok + b * BLK + lax.broadcasted_iota(jnp.int32, (BLK, nq), 0)
        scores = jnp.where(token <= limit, scores, NEG)
        top = jnp.max(scores, axis=0, keepdims=True)
        expo = jnp.exp(scores - top)
        ex[at, :] = expo
        tot = jnp.sum(expo, axis=0, keepdims=True)
        for j in range(nq // 128):
            stat[b, j : j + 1, :] = top[:, j * 128 : (j + 1) * 128]
            stat[b, 4 + j : 5 + j, :] = tot[:, j * 128 : (j + 1) * 128]

    for b in range(nb):
        for k in range(b * per, (b + 1) * per):
            landed(3, k)
            go(send(hbuf.at[3, part(k)], 7, k, d2d_send.at[2, k], partner))
        accumulate(3, b * BLK, 1, BLK)
        for k in range(b * per, (b + 1) * per):
            landed(7, k)
        accumulate(7, b * BLK, 1, BLK)
        finish(b)

    merged = stat[0]
    for b in range(1, nb):
        other = stat[b]
        top = jnp.maximum(merged, other)
        scaled = pltpu.roll(jnp.exp(merged - top), 4, 0) * merged + pltpu.roll(jnp.exp(other - top), 4, 0) * other
        sub = lax.broadcasted_iota(jnp.int32, (8, 128), 0)
        merged = jnp.where(sub < 4, top, scaled)
    stat_recv[s] = merged

    def peer(d):
        return {"seq": lax.rem(y + d // n_z, n_y) * n_z + lax.rem(z + d % n_z, n_z), "head": h}

    def stat_copy(d):
        return pltpu.make_async_remote_copy(
            src_ref=stat_recv.at[s], dst_ref=stat_recv.at[s], send_sem=stat_ssem.at[d],
            recv_sem=stat_rsem.at[d], device_id=peer(d), device_id_type=MESH,
        )

    def blk_copy(d):
        return pltpu.make_async_remote_copy(
            src_ref=blk_recv.at[s, 0:1], dst_ref=blk_recv.at[s, 0:1], send_sem=blk_ssem.at[d],
            recv_sem=blk_rsem.at[d], device_id=peer(d), device_id_type=MESH,
        )

    def distance(d):
        dy, dz = d // n_z, d % n_z
        return min(dy, n_y - dy) + min(dz, n_z - dz)

    peers = sorted(range(1, n_seq), key=lambda d: (-distance(d), d))

    def each_peer(act):
        for d in peers:
            act(d)

    each_peer(lambda d: stat_copy(d).start())

    halo_copy(0, seq_prev).wait_recv()
    halo_copy(1, seq_next).wait_recv()
    edge_keys = jnp.concatenate([halo_recv[0, 0], halo_recv[1, 0]], axis=0).astype(jnp.bfloat16)
    edge_scores = scores_of(edge_keys)
    edge_row = lax.broadcasted_iota(jnp.int32, (32, nq), 0)
    edge_token = jnp.where(edge_row < 16, (s + 1) * tok + edge_row, s * tok - 32 + edge_row)
    edge_ok = (edge_token >= 0) & (edge_token <= limit)
    edge_scores = jnp.where(edge_ok, edge_scores, NEG)
    edge_top = jnp.max(edge_scores, axis=0, keepdims=True)
    edge_expo = jnp.where(edge_ok, jnp.exp(edge_scores - edge_top), 0.0)
    for j in range(nq // 128):
        stat[nb, j : j + 1, :] = edge_top[:, j * 128 : (j + 1) * 128]

    ext[...] = jnp.zeros_like(ext)
    halo_p[...] = jnp.zeros_like(halo_p)
    each_peer(lambda d: stat_copy(d).wait_recv())
    everyone = stat_recv[...]
    row_top = jnp.max(everyone, axis=0)
    row_total = jnp.sum(pltpu.roll(jnp.exp(everyone - row_top[None]), 4, 1) * everyone, axis=0)
    row_total = pltpu.roll(row_total, 4, 0)
    sub8 = lax.broadcasted_iota(jnp.int32, (8, 128), 0)
    lane8 = lax.broadcasted_iota(jnp.int32, (8, 128), 1)
    wrow = lax.rem(lane8, window)
    used = (wrow >= window - wlen[0]) & (sub8 < 4)
    for b in range(nb + 1):
        factor = jnp.exp(stat[b] - row_top) / row_total
        gt[b] = jnp.where(used, factor, 0.0)

    def weighted(expo, b):
        total = expo[:, 0:128] * gt[b, 0:1, :]
        for j in range(1, nq // 128):
            total = total + expo[:, j * 128 : (j + 1) * 128] * gt[b, j : j + 1, :]
        return total

    for b in range(nb):
        at = slice(b * BLK, (b + 1) * BLK)
        column = weighted(ex[at, :], b) * vmag[at, :]
        ext[b + 1 : b + 2, :] = jnp.sum(column.T, axis=0, keepdims=True)
    edge = weighted(edge_expo, nb)
    halo_p[0:16, :] = edge[0:16, :] * halo_recv[0, 1]
    halo_p[BLK - 16 :, :] = edge[16:32, :] * halo_recv[1, 1]
    edge_row_sum = jnp.sum(halo_p[...].T, axis=0, keepdims=True)
    ext[0:1, :] = edge_row_sum
    ext[nb + 1 : nb + 2, :] = edge_row_sum

    here = ext[...]
    before = pltpu.roll(here, 1, 0)
    after = pltpu.roll(here, 7, 0)
    halfspan = (kwidth[0] - 1) // 2
    pooled = here
    for shift in range(1, (KERNEL_LIMIT - 1) // 2 + 1):
        ahead = pltpu.roll(jnp.where(lane8 >= shift, here, after), 128 - shift, 1)
        behind = pltpu.roll(jnp.where(lane8 < 128 - shift, here, before), shift, 1)
        wider = jnp.maximum(jnp.maximum(pooled, ahead), behind)
        pooled = jnp.where(shift <= halfspan, wider, pooled)
    sums = jnp.broadcast_to(jnp.sum(pooled, axis=1, keepdims=True), (8, 128))
    mine = (sub8 >= 1) & (sub8 <= nb)
    local = jnp.sum(jnp.where(mine & (lane8 == sub8 - 1), sums, 0.0), axis=0, keepdims=True)
    placed = jnp.sum(jnp.where(mine & (lane8 == s * nb + sub8 - 1), sums, 0.0), axis=0, keepdims=True)
    blk_recv[s, 0:1, :] = placed
    each_peer(lambda d: blk_copy(d).start())
    each_peer(lambda d: blk_copy(d).wait_recv())
    row = jnp.sum(blk_recv[:, 0:1, :], axis=0)
    by_lane = jnp.broadcast_to(row, (128, 128))
    by_sub = by_lane.T
    si = lax.broadcasted_iota(jnp.int32, (128, 128), 0)
    li = lax.broadcasted_iota(jnp.int32, (128, 128), 1)
    larger = (by_sub > by_lane) | ((by_sub == by_lane) & (si < li))
    rank = jnp.sum(larger.astype(jnp.float32), axis=0, keepdims=True)
    kept = jnp.sum(jnp.where(rank < keep[0].astype(jnp.float32), row, 0.0), axis=1, keepdims=True)
    fraction = kept / jnp.sum(row, axis=1, keepdims=True)
    lane1 = lax.broadcasted_iota(jnp.int32, (1, 128), 1)
    out[...] = jnp.where(lane1 < nb, local, fraction)

    for cp in started:
        cp.wait_send()
    each_peer(lambda d: stat_copy(d).wait_send())
    each_peer(lambda d: blk_copy(d).wait_send())


def split_kernel(joined, blocks, frac):
    nb = blocks.shape[1]
    blocks[...] = joined[:, 0:nb]
    frac[...] = joined[:, nb : nb + 1]


def solution(mesh):
    n_seq = mesh.shape["seq"]

    def local(hidden, gain, key_matrix, value_matrix, queries, window_len, kernel_width, kept_block_count):
        tok, feat = hidden.shape
        width, hd = key_matrix.shape
        nq = queries.shape[0] * queries.shape[1] // hd
        nb = tok // BLK
        freq = (500000.0 ** (-(np.arange(hd // 2) * 2.0) / hd)).astype(np.float32)
        freq = jnp.asarray(np.concatenate([freq, freq])[None, :])
        anyspace = pl.BlockSpec(memory_space=pl.ANY)
        vmem = pl.BlockSpec(memory_space=pltpu.VMEM)
        smem = pl.BlockSpec(memory_space=pltpu.SMEM)
        f32, bf16 = jnp.float32, jnp.bfloat16
        dma = pltpu.SemaphoreType.DMA
        joined = pl.pallas_call(
            functools.partial(kernel, n_seq),
            out_shape=jax.ShapeDtypeStruct((1, 128), f32),
            in_specs=[anyspace] * 5 + [smem] * 3 + [anyspace],
            out_specs=vmem,
            scratch_shapes=[
                pltpu.VMEM((8, tok, feat), bf16),
                pltpu.VMEM((width, 2 * hd), bf16),
                pltpu.VMEM((1, width), f32),
                pltpu.VMEM(queries.shape, bf16),
                pltpu.VMEM((1, hd), f32),
                pltpu.VMEM((nq, hd), bf16),
                pltpu.VMEM((hd, nq), bf16),
                pltpu.VMEM((tok, hd), f32),
                pltpu.VMEM((tok, hd), f32),
                pltpu.VMEM((tok, 2 * hd), f32),
                pltpu.VMEM((tok, 128), f32),
                pltpu.VMEM((tok, 128), f32),
                pltpu.VMEM((tok, nq), f32),
                pltpu.VMEM((nb + 1, 8, 128), f32),
                pltpu.VMEM((nb + 1, 8, 128), f32),
                pltpu.VMEM((8, 128), f32),
                pltpu.VMEM((BLK, 128), f32),
                pltpu.VMEM((2, 2, 16, 128), f32),
                pltpu.VMEM((2, 2, 16, 128), f32),
                pltpu.VMEM((n_seq, 8, 128), f32),
                pltpu.VMEM((n_seq, 8, 128), f32),
                dma((6,)),
                dma((2, CHUNKS)),
                dma((CHUNKS,)),
                dma((CHUNKS,)),
                dma((3, CHUNKS)),
                dma((8, CHUNKS)),
                dma((2,)),
                dma((2,)),
                dma((n_seq,)),
                dma((n_seq,)),
                dma((n_seq,)),
                dma((n_seq,)),
                pltpu.SemaphoreType.REGULAR((N_Z // 2 - 1 + n_seq // N_Z // 2,)),
            ],
            compiler_params=pltpu.CompilerParams(
                collective_id=0, has_side_effects=True, vmem_limit_bytes=56 * 1024 * 1024
            ),
        )(
            hidden, gain.reshape(1, -1), key_matrix, value_matrix, queries,
            window_len, kernel_width, kept_block_count, freq,
        )
        blocks, frac = pl.pallas_call(
            split_kernel,
            out_shape=(jax.ShapeDtypeStruct((1, nb), f32), jax.ShapeDtypeStruct((1, 1), f32)),
            in_specs=[vmem],
            out_specs=(vmem, vmem),
        )(joined)
        return blocks, frac.reshape(1)

    return jax.shard_map(
        local,
        mesh=mesh,
        in_specs=(
            P("seq", "head"), P(), P(None, "head"), P(None, "head"), P(None, "head"),
            P("head"), P("head"), P("head"),
        ),
        out_specs=(P("head", "seq"), P("head")),
        check_vma=False,
    )
```
